32 devices in a mesh: dp: 8 (over y, x, core), shard: 4 (over z).
Axes of the slice: x: 2, y: 2, z: 4, core: 2. Of those that a mesh axis runs over, the one named last changes fastest.
Arguments:
- x_in: bfloat16 [4096, 1024], P(('dp', 'shard')), may hold values from -6 to 6
- cotangent: float32 [4096, 1024], P(('dp', 'shard')), may hold values from -6 to 6
- params: float32 [12595200], P(('dp', 'shard')), may hold values from -2 to 2
- first_moment: float32 [12595200], P(('dp', 'shard')), may hold values from -6 to 6
- second_moment: float32 [12595200], P(('dp', 'shard')), may hold values from 0.01 to 1
- seq_lengths: int32 [128], replicated, may hold values from 1 to 125, as said below
- seq_device: int32 [128], replicated, may hold values from 0 to 31, as said below
Outputs:
- block_out: float32 [4096, 1024], P(('dp', 'shard'))
- x_grad: float32 [4096, 1024], P(('dp', 'shard'))
- grad_flat: float32 [12595200], P(('dp', 'shard'))
- new_params: float32 [12595200], P(('dp', 'shard'))
- new_first: float32 [12595200], P(('dp', 'shard'))
- new_second: float32 [12595200], P(('dp', 'shard'))
The draws below stay inside these ranges and needn't reach their ends.
Inputs may be any that keep to these rules, and one draw needn't show every extreme that they name: `seq_lengths`: every device holds exactly 4 sequences of together at most 128 tokens; some device holds exactly 128. `seq_device`: every device index names exactly 4 sequences.
All inputs are finite; a program needn't handle non-finite values.
Results may differ from the reference program's by a relative error of at most 0.024.
The reference program's roundings to bfloat16 on the way count: a program that leaves them out, or rounds other values in their place, can miss the bound.
Values may be sent and summed in bfloat16 or wider, within the bound.
No kernel may reach another device: no remote copies, remote signals or barrier semaphores. Data moves between devices by JAX's collectives and lax.ppermute only.
A program may use at most 256 MiB of HBM per device.

```python
import math
import jax
import jax.numpy as jnp
from jax import lax

D = 1024
HEADS = 16
HEAD_DIM = 64
FF = 4096
ROWS_DEV = 128
STEP = 4
SEQ_DEV = 4
TOKENS = 4096
NSEQ = 128
NPARAM = 12595200
N_DP = 8
N_SHARD = 4


def packing(key):
    device_total = NSEQ // SEQ_DEV
    key_total, key_full, key_cuts, key_order = jax.random.split(jax.random.fold_in(key, 11), 4)
    totals = jax.random.randint(key_total, (device_total,), ROWS_DEV // 4 + SEQ_DEV, ROWS_DEV + 1).astype(jnp.int32)
    full_device = jax.random.randint(key_full, (), 0, device_total).astype(jnp.int32)
    device_ids = jnp.arange(device_total, dtype=jnp.int32)
    totals = jnp.where(device_ids == full_device, ROWS_DEV, totals).astype(jnp.int32)
    raw_cuts = jax.random.randint(key_cuts, (device_total, SEQ_DEV - 1), 0, 1 << 20).astype(jnp.int32)
    cuts = jnp.sort(jnp.remainder(raw_cuts, totals[:, None] - SEQ_DEV + 1), axis=1)
    zero_col = jnp.zeros((device_total, 1), jnp.int32)
    bounds = jnp.concatenate([zero_col, cuts, (totals - SEQ_DEV)[:, None]], axis=1)
    lengths = bounds[:, 1:] - bounds[:, :-1] + 1
    longest = jnp.concatenate([jnp.full((1,), ROWS_DEV - SEQ_DEV + 1, jnp.int32), jnp.ones((SEQ_DEV - 1,), jnp.int32)])
    lengths = jnp.where((device_ids == full_device)[:, None], longest[None, :], lengths).astype(jnp.int32)
    owners = jnp.repeat(device_ids, SEQ_DEV)
    order = jax.random.permutation(key_order, NSEQ)
    return (lengths.reshape(NSEQ)[order], owners[order])


def draw_seq_lengths(key, part):
    return packing(key)[0]


def draw_seq_device(key, part):
    return packing(key)[1]


def rough(key, target, factor):
    base = jnp.clip(jax.random.normal(key, target, jnp.float32), -4.0, 4.0)
    return base * factor


def arrange(pieces, devices):
    share = D // devices
    vec_rows = 8 + FF // D
    columns = [piece.reshape(devices, -1) for piece in pieces[:4]]
    columns.append(jnp.transpose(pieces[4].reshape(vec_rows, devices, share), (1, 0, 2)).reshape(devices, vec_rows * share))
    return jnp.concatenate(columns, axis=1).reshape(-1)


def draw_params(key, part):
    devices = NSEQ // SEQ_DEV
    keys = jax.random.split(jax.random.fold_in(key, 5), 16)
    width_scale = D ** (-0.5)
    query_base = rough(keys[0], (D, D), 1.0)
    fresh_part = rough(keys[1], (D, D), 1.0)
    query_part = query_base * width_scale
    key_part = fresh_part * width_scale
    value_part = rough(keys[3], (D, D), width_scale)
    qkv_weight = jnp.concatenate([query_part, key_part, value_part], axis=1)
    out_weight = rough(keys[4], (D, D), 3.0 * width_scale)
    up_weight = rough(keys[5], (D, FF), width_scale)
    down_weight = rough(keys[6], (FF, D), FF ** (-0.5))
    first_gain = 1.0 + 0.3 * jax.random.uniform(keys[7], (D,), jnp.float32, -1.0, 1.0)
    first_shift = rough(keys[8], (D,), 0.2)
    query_bias = rough(keys[9], (D,), 0.2)
    value_bias = rough(keys[10], (D,), 0.2)
    out_bias = rough(keys[11], (D,), 0.2)
    second_gain = 1.0 + 0.3 * jax.random.uniform(keys[12], (D,), jnp.float32, -1.0, 1.0)
    second_shift = rough(keys[13], (D,), 0.2)
    up_bias = rough(keys[14], (FF,), 0.2)
    down_bias = rough(keys[15], (D,), 0.2)
    vectors = jnp.concatenate([jnp.stack([first_gain, first_shift, query_bias, value_bias, out_bias, second_gain, second_shift]), up_bias.reshape(FF // D, D), down_bias[None, :]], axis=0)
    return arrange((qkv_weight, out_weight, up_weight, down_weight, vectors), devices).astype(jnp.float32)


def spiked(result, own_key, source, target, parts, factor):
    def block_of(dim):
        return (jnp.arange(result.shape[dim]) // (result.shape[dim] // parts)).reshape((-1,) + (1,) * (result.ndim - 1 - dim))

    near = jax.random.permutation(own_key, parts)[block_of(target)]
    far = (block_of(target) + parts // 2) % parts
    return jnp.where((block_of(source) == near) | (block_of(source) == far), factor * result, result)


def level_of(own_key, dims, cuts, smallest, high):
    level, own = 1.0, jax.random.fold_in(own_key, 6)
    for dim, parts in cuts:
        steps = jnp.exp(jax.random.uniform(jax.random.fold_in(own, dim), (parts,), jnp.float32, smallest / len(cuts), high / len(cuts)))
        level = level * jnp.repeat(steps, dims[dim] // parts).reshape([-1 if axis == dim else 1 for axis in range(len(dims))])
    return level


def noise(own_key, shape, width, reach, cuts=(), kind=jnp.bfloat16):
    drawn = width * jax.random.normal(own_key, shape, jnp.float32)
    if cuts:
        drawn = drawn * level_of(own_key, shape, cuts, -0.22, 0.18)
    return jnp.clip(drawn, -reach, reach).astype(kind)


def noise_with(key, dims, width, most, shards, heavy, kind=jnp.bfloat16):
    values = width * jax.random.normal(key, dims, jnp.float32)
    if shards:
        values = values * level_of(key, dims, shards, -0.22, 0.18)
    return jnp.clip(spiked(values, jax.random.fold_in(key, 3), *heavy), -most, most).astype(kind)


def setup_inputs(seed: int = 0) -> dict:
    splits = jax.random.split(jax.random.key(seed), 8)
    x_in = noise(splits[0], (TOKENS, D), 1.0, 6.0, ((0, 32),))
    cotangent = noise_with(splits[1], (TOKENS, D), 1.0, 6.0, ((0, 32),), (0, 1, 32, 2.75), jnp.float32)
    params = draw_params(jax.random.fold_in(splits[7], 71), 0)
    first_moment = noise(splits[3], (NPARAM,), 1.0, 6.0, ((0, 32),), jnp.float32)
    second_moment = jnp.clip(jnp.exp(math.log(1.0) - 4.6051702 * jax.random.uniform(splits[4], (NPARAM,), jnp.float32) ** level_of(splits[4], (NPARAM,), ((0, 32),), -0.2, 0.2)), 0.01, 1.0)
    seq_lengths = draw_seq_lengths(jax.random.fold_in(splits[7], 71), 0)
    seq_device = draw_seq_device(jax.random.fold_in(splits[7], 71), 0)
    return dict(x_in=x_in, cotangent=cotangent, params=params, first_moment=first_moment, second_moment=second_moment, seq_lengths=seq_lengths, seq_device=seq_device)


score_scale = 0.125
norm_eps = 1e-05
gelu_coef = 0.7978845608028654
gelu_cubic = 0.044715
learn_rate = 0.01
beta_first = 0.9
beta_second = 0.95
adam_eps = 1e-08
decay_rate = 0.1
neg_large = -1e+30

def split_layout(flat_vector, devices):
    per_device = flat_vector.shape[0] // devices
    share = D // devices
    vec_rows = 8 + FF // D
    table = flat_vector.reshape(devices, per_device)
    widths = [share * 3 * D, share * D, share * FF, share * FF, vec_rows * share]
    pieces = []
    offset = 0
    for extent in widths:
        pieces.append(table[:, offset:offset + extent])
        offset = offset + extent
    qkv_weight = pieces[0].reshape(D, 3 * D)
    out_weight = pieces[1].reshape(D, D)
    up_weight = pieces[2].reshape(D, FF)
    down_weight = pieces[3].reshape(FF, D)
    vectors = jnp.transpose(pieces[4].reshape(devices, vec_rows, share), (1, 0, 2)).reshape(vec_rows, D)
    return (qkv_weight, out_weight, up_weight, down_weight, vectors)

def join_layout(pieces, devices):
    share = D // devices
    vec_rows = 8 + FF // D
    columns = [piece.reshape(devices, -1) for piece in pieces[:4]]
    columns.append(jnp.transpose(pieces[4].reshape(vec_rows, devices, share), (1, 0, 2)).reshape(devices, vec_rows * share))
    return jnp.concatenate(columns, axis=1).reshape(-1)

def matmul(left_side, right_side):
    return jnp.dot(left_side, right_side, preferred_element_type=jnp.float32)

def matmul_tn(left_side, right_side):
    return lax.dot_general(left_side, right_side, (((0,), (0,)), ((), ())), preferred_element_type=jnp.float32)

def matmul_nt(left_side, right_side):
    return lax.dot_general(left_side, right_side, (((1,), (1,)), ((), ())), preferred_element_type=jnp.float32)

def contract(pattern, left_side, right_side):
    return jnp.einsum(pattern, left_side.astype(jnp.float32), right_side.astype(jnp.float32))

def normalize(values, norm_gain, norm_shift):
    average = lax.optimization_barrier(jnp.mean(values, axis=-1, keepdims=True))
    centered = values - average
    inverse = lax.rsqrt(lax.optimization_barrier(jnp.mean(centered * centered, axis=-1, keepdims=True)) + norm_eps)
    scaled = centered * inverse
    return (scaled * norm_gain + norm_shift, scaled, inverse)

def normalize_back(upstream, scaled, inverse, norm_gain):
    grad_scaled = upstream * norm_gain
    term_one = lax.optimization_barrier(jnp.mean(grad_scaled, axis=-1, keepdims=True))
    term_two = lax.optimization_barrier(jnp.mean(grad_scaled * scaled, axis=-1, keepdims=True))
    return inverse * (grad_scaled - term_one - scaled * term_two)

def gelu_parts(pre_act):
    inner_arg = gelu_coef * (pre_act + gelu_cubic * pre_act * pre_act * pre_act)
    tanh_val = jnp.tanh(inner_arg)
    act_value = 0.5 * pre_act * (1.0 + tanh_val)
    act_slope = 0.5 * (1.0 + tanh_val) + 0.5 * pre_act * (1.0 - tanh_val * tanh_val) * gelu_coef * (1.0 + 3.0 * gelu_cubic * pre_act * pre_act)
    return (act_value, act_slope)

def segments(seq_lengths, seq_device, device_ids, row_count):
    owned = seq_device[None, :] == device_ids[:, None]
    own_lengths = jnp.where(owned, seq_lengths[None, :], 0).astype(jnp.int32)
    ends = jnp.cumsum(own_lengths, axis=1).astype(jnp.int32)
    position = jnp.arange(row_count, dtype=jnp.int32)
    passed = owned[:, None, :] & (ends[:, None, :] <= position[None, :, None])
    seg_ids = lax.optimization_barrier(jnp.sum(passed.astype(jnp.int32), axis=2)).astype(jnp.int32)
    live_mask = position[None, :] < ends[:, -1:]
    return (seg_ids, live_mask)

def layer(x_in, cotangent, seg_ids, live_mask, weights):
    qkv_weight, out_weight, up_weight, down_weight, vectors = weights
    vectors = vectors.astype(jnp.float32)
    first_gain = vectors[0]
    first_shift = vectors[1]
    query_bias = vectors[2]
    value_bias = vectors[3]
    out_bias = vectors[4]
    second_gain = vectors[5]
    second_shift = vectors[6]
    up_bias = vectors[7:7 + FF // D].reshape(FF)
    down_bias = vectors[7 + FF // D]
    batch_size = x_in.shape[0]
    row_count = x_in.shape[1]
    flat_rows = batch_size * row_count
    head_shape = (batch_size, row_count, HEADS, HEAD_DIM)
    stream = x_in.astype(jnp.float32).reshape(flat_rows, D)
    normed1, scaled1, inverse1 = normalize(stream, first_gain, first_shift)
    normed1 = normed1.astype(jnp.bfloat16)
    mixed_all = matmul(normed1, qkv_weight)
    query_low = (mixed_all[:, :D] + query_bias).astype(jnp.bfloat16).reshape(head_shape)
    key_low = mixed_all[:, D:2 * D].astype(jnp.bfloat16).reshape(head_shape)
    value_low = (mixed_all[:, 2 * D:] + value_bias).astype(jnp.bfloat16).reshape(head_shape)
    position = jnp.arange(row_count, dtype=jnp.int32)
    allowed = (seg_ids[:, :, None] == seg_ids[:, None, :]) & (position[None, :, None] >= position[None, None, :])
    allowed = allowed[:, None, :, :]
    scores = jnp.where(allowed, contract('bqhe,bkhe->bhqk', query_low, key_low) * score_scale, neg_large)
    row_max = lax.optimization_barrier(jnp.max(scores, axis=-1, keepdims=True))
    exp_scores = jnp.exp(scores - row_max)
    row_total = lax.optimization_barrier(jnp.sum(exp_scores, axis=-1, keepdims=True))
    probability = exp_scores / row_total
    log_total = row_max + jnp.log(row_total)
    attended = contract('bhqk,bkhe->bqhe', probability.astype(jnp.bfloat16), value_low)
    attended = attended.astype(jnp.bfloat16).reshape(flat_rows, D)
    residual = stream + matmul(attended, out_weight) + out_bias
    normed2, scaled2, inverse2 = normalize(residual, second_gain, second_shift)
    normed2 = normed2.astype(jnp.bfloat16)
    pre_act = matmul(normed2, up_weight) + up_bias
    act_value, act_slope = gelu_parts(pre_act)
    hidden = act_value.astype(jnp.bfloat16)
    output = residual + matmul(hidden, down_weight) + down_bias
    upstream = cotangent.reshape(flat_rows, D) * live_mask.reshape(flat_rows, 1).astype(jnp.float32)
    up_low = upstream.astype(jnp.bfloat16)
    grad_down = matmul_tn(hidden, up_low)
    grad_pre = matmul_nt(up_low, down_weight) * act_slope
    pre_low = grad_pre.astype(jnp.bfloat16)
    grad_up = matmul_tn(normed2, pre_low)
    grad_normed2 = matmul_nt(pre_low, up_weight)
    grad_residual = upstream + normalize_back(grad_normed2, scaled2, inverse2, second_gain)
    res_low = grad_residual.astype(jnp.bfloat16)
    grad_out = matmul_tn(attended, res_low)
    grad_attended = matmul_nt(res_low, out_weight).astype(jnp.bfloat16).reshape(head_shape)
    scores = jnp.where(allowed, contract('bqhe,bkhe->bhqk', query_low, key_low) * score_scale, neg_large)
    probability = jnp.where(allowed, jnp.exp(scores - log_total), 0.0)
    grad_prob = contract('bqhe,bkhe->bhqk', grad_attended, value_low)
    grad_values = contract('bhqk,bqhe->bkhe', probability.astype(jnp.bfloat16), grad_attended)
    row_dot = lax.optimization_barrier(jnp.sum(probability * grad_prob, axis=-1, keepdims=True))
    score_low = (probability * (grad_prob - row_dot)).astype(jnp.bfloat16)
    grad_queries = contract('bhqk,bkhe->bqhe', score_low, key_low) * score_scale
    grad_keys = contract('bhqk,bqhe->bkhe', score_low, query_low) * score_scale
    grad_queries = grad_queries.reshape(flat_rows, D)
    grad_keys = grad_keys.reshape(flat_rows, D)
    grad_values = grad_values.reshape(flat_rows, D)
    mixed_low = jnp.concatenate([grad_queries, grad_keys, grad_values], axis=1).astype(jnp.bfloat16)
    grad_qkv = matmul_tn(normed1, mixed_low)
    grad_normed1 = matmul_nt(mixed_low, qkv_weight)
    grad_input = grad_residual + normalize_back(grad_normed1, scaled1, inverse1, first_gain)
    head_rows = jnp.stack([lax.optimization_barrier(jnp.sum(grad_normed1 * scaled1, axis=0)), lax.optimization_barrier(jnp.sum(grad_normed1, axis=0)), lax.optimization_barrier(jnp.sum(grad_queries, axis=0)), lax.optimization_barrier(jnp.sum(grad_values, axis=0)), lax.optimization_barrier(jnp.sum(grad_residual, axis=0)), lax.optimization_barrier(jnp.sum(grad_normed2 * scaled2, axis=0)), lax.optimization_barrier(jnp.sum(grad_normed2, axis=0))])
    grad_vectors = jnp.concatenate([head_rows, lax.optimization_barrier(jnp.sum(grad_pre, axis=0)).reshape(FF // D, D), lax.optimization_barrier(jnp.sum(upstream, axis=0))[None, :]], axis=0)
    grads = (grad_qkv, grad_out, grad_up, grad_down, grad_vectors)
    return (output.reshape(batch_size, row_count, D), grad_input.reshape(batch_size, row_count, D), grads)

def reference(x_in, cotangent, params, first_moment, second_moment, seq_lengths, seq_device):
    devices = N_DP * N_SHARD
    weights = split_layout(params.astype(jnp.bfloat16), devices)
    device_total = TOKENS // ROWS_DEV
    per_block = math.gcd(device_total, max(1, 4096 // ROWS_DEV))
    block_count = device_total // per_block
    x_blocks = x_in.reshape(block_count, per_block, ROWS_DEV, D)
    cot_blocks = cotangent.reshape(block_count, per_block, ROWS_DEV, D)

    def visit(running, inputs):
        x_part, cot_part, block_index = inputs
        device_ids = (block_index * per_block + jnp.arange(per_block, dtype=jnp.int32)).astype(jnp.int32)
        seg_ids, live_mask = segments(seq_lengths, seq_device, device_ids, ROWS_DEV)
        output, grad_input, grads = layer(x_part, cot_part, seg_ids, live_mask, weights)
        return (jax.tree.map(lambda left, right: left + right, running, grads), (output, grad_input))
    start_grads = (jnp.zeros((D, 3 * D), jnp.float32), jnp.zeros((D, D), jnp.float32), jnp.zeros((D, FF), jnp.float32), jnp.zeros((FF, D), jnp.float32), jnp.zeros((8 + FF // D, D), jnp.float32))
    grad_parts, (outputs, grad_inputs) = lax.scan(visit, start_grads, (x_blocks, cot_blocks, jnp.arange(block_count, dtype=jnp.int32)))
    grads = join_layout(grad_parts, devices)
    per_device = NPARAM // devices
    share = D // devices
    local_index = jnp.arange(per_device, dtype=jnp.int32)
    matrix_mask = jnp.broadcast_to((local_index < share * (4 * D + 2 * FF)).astype(jnp.float32)[None, :], (devices, per_device)).reshape(-1)
    new_first = beta_first * first_moment + (1.0 - beta_first) * grads
    new_second = beta_second * second_moment + (1.0 - beta_second) * grads * grads
    fix_first = 1.0 - beta_first ** STEP
    fix_second = 1.0 - beta_second ** STEP
    ratio = new_first / fix_first / (jnp.sqrt(new_second / fix_second) + adam_eps)
    new_params = params - learn_rate * (ratio + decay_rate * matrix_mask * params)
    return (outputs.reshape(TOKENS, D), grad_inputs.reshape(TOKENS, D), grads, new_params, new_first, new_second)
```

```python
import jax
import jax.numpy as jnp
from jax import lax
from jax.sharding import Mesh
from jax.sharding import PartitionSpec as P

D = 1024
HEADS = 16
HEAD_DIM = 64
FF = 4096
STEP = 4


score_scale = 0.125
norm_eps = 1e-05
gelu_coef = 0.7978845608028654
gelu_cubic = 0.044715
learn_rate = 0.01
beta_first = 0.9
beta_second = 0.95
adam_eps = 1e-08
decay_rate = 0.1
neg_large = -1e30


def matmul(left_side, right_side):
    return jnp.dot(left_side, right_side, preferred_element_type=jnp.float32)


def matmul_tn(left_side, right_side):
    return lax.dot_general(
        left_side, right_side, (((0,), (0,)), ((), ())), preferred_element_type=jnp.float32
    )


def matmul_nt(left_side, right_side):
    return lax.dot_general(
        left_side, right_side, (((1,), (1,)), ((), ())), preferred_element_type=jnp.float32
    )


def contract(pattern, left_side, right_side):
    return jnp.einsum(pattern, left_side, right_side, preferred_element_type=jnp.float32)


def normalize(values, norm_gain, norm_shift):
    average = jnp.mean(values, axis=-1, keepdims=True)
    centered = values - average
    inverse = lax.rsqrt(jnp.mean(centered * centered, axis=-1, keepdims=True) + norm_eps)
    scaled = centered * inverse
    return (scaled * norm_gain + norm_shift, scaled, inverse)


def normalize_back(upstream, scaled, inverse, norm_gain):
    grad_scaled = upstream * norm_gain
    term_one = jnp.mean(grad_scaled, axis=-1, keepdims=True)
    term_two = jnp.mean(grad_scaled * scaled, axis=-1, keepdims=True)
    return inverse * (grad_scaled - term_one - scaled * term_two)


def gelu_parts(pre_act):
    inner_arg = gelu_coef * (pre_act + gelu_cubic * pre_act * pre_act * pre_act)
    tanh_val = jnp.tanh(inner_arg)
    act_value = 0.5 * pre_act * (1.0 + tanh_val)
    act_slope = 0.5 * (1.0 + tanh_val) + 0.5 * pre_act * (1.0 - tanh_val * tanh_val) * gelu_coef * (
        1.0 + 3.0 * gelu_cubic * pre_act * pre_act
    )
    return (act_value, act_slope)


def segments(seq_lengths, seq_device, device_ids, row_count):
    owned = seq_device[None, :] == device_ids[:, None]
    own_lengths = jnp.where(owned, seq_lengths[None, :], 0)
    ends = jnp.cumsum(own_lengths, axis=1)
    position = jnp.arange(row_count, dtype=jnp.int32)
    passed = owned[:, None, :] & (ends[:, None, :] <= position[None, :, None])
    seg_ids = jnp.sum(passed.astype(jnp.int32), axis=2)
    live_mask = position[None, :] < ends[:, -1:]
    return (seg_ids, live_mask)


def layer(x_in, cotangent, seg_ids, live_mask, weights):
    qkv_weight, out_weight, up_weight, down_weight, vectors = weights
    vectors = vectors.astype(jnp.float32)
    first_gain = vectors[0]
    first_shift = vectors[1]
    query_bias = vectors[2]
    value_bias = vectors[3]
    out_bias = vectors[4]
    second_gain = vectors[5]
    second_shift = vectors[6]
    up_bias = vectors[7 : 7 + FF // D].reshape(FF)
    down_bias = vectors[7 + FF // D]
    batch_size = x_in.shape[0]
    row_count = x_in.shape[1]
    flat_rows = batch_size * row_count
    head_shape = (batch_size, row_count, HEADS, HEAD_DIM)
    stream = x_in.astype(jnp.float32).reshape(flat_rows, D)
    normed1, scaled1, inverse1 = normalize(stream, first_gain, first_shift)
    normed1 = normed1.astype(jnp.bfloat16)
    mixed_all = matmul(normed1, qkv_weight)
    query_low = (mixed_all[:, :D] + query_bias).astype(jnp.bfloat16).reshape(head_shape)
    key_low = mixed_all[:, D : 2 * D].astype(jnp.bfloat16).reshape(head_shape)
    value_low = (mixed_all[:, 2 * D :] + value_bias).astype(jnp.bfloat16).reshape(head_shape)
    position = jnp.arange(row_count, dtype=jnp.int32)
    allowed = (seg_ids[:, :, None] == seg_ids[:, None, :]) & (
        position[None, :, None] >= position[None, None, :]
    )
    allowed = allowed[:, None, :, :]
    scores = jnp.where(
        allowed, contract("bqhe,bkhe->bhqk", query_low, key_low) * score_scale, neg_large
    )
    row_max = jnp.max(scores, axis=-1, keepdims=True)
    exp_scores = jnp.exp(scores - row_max)
    row_total = jnp.sum(exp_scores, axis=-1, keepdims=True)
    probability = exp_scores / row_total
    log_total = row_max + jnp.log(row_total)
    attended = contract("bhqk,bkhe->bqhe", probability.astype(jnp.bfloat16), value_low)
    attended = attended.astype(jnp.bfloat16).reshape(flat_rows, D)
    residual = stream + matmul(attended, out_weight) + out_bias
    normed2, scaled2, inverse2 = normalize(residual, second_gain, second_shift)
    normed2 = normed2.astype(jnp.bfloat16)
    pre_act = matmul(normed2, up_weight) + up_bias
    act_value, act_slope = gelu_parts(pre_act)
    hidden = act_value.astype(jnp.bfloat16)
    output = residual + matmul(hidden, down_weight) + down_bias
    upstream = cotangent.reshape(flat_rows, D) * live_mask.reshape(flat_rows, 1).astype(jnp.float32)
    up_low = upstream.astype(jnp.bfloat16)
    grad_down = matmul_tn(hidden, up_low)
    grad_pre = matmul_nt(up_low, down_weight) * act_slope
    pre_low = grad_pre.astype(jnp.bfloat16)
    grad_up = matmul_tn(normed2, pre_low)
    grad_normed2 = matmul_nt(pre_low, up_weight)
    grad_residual = upstream + normalize_back(grad_normed2, scaled2, inverse2, second_gain)
    res_low = grad_residual.astype(jnp.bfloat16)
    grad_out = matmul_tn(attended, res_low)
    grad_attended = matmul_nt(res_low, out_weight).astype(jnp.bfloat16).reshape(head_shape)
    scores = jnp.where(
        allowed, contract("bqhe,bkhe->bhqk", query_low, key_low) * score_scale, neg_large
    )
    probability = jnp.where(allowed, jnp.exp(scores - log_total), 0.0)
    grad_prob = contract("bqhe,bkhe->bhqk", grad_attended, value_low)
    grad_values = contract("bhqk,bqhe->bkhe", probability.astype(jnp.bfloat16), grad_attended)
    row_dot = jnp.sum(probability * grad_prob, axis=-1, keepdims=True)
    score_low = (probability * (grad_prob - row_dot)).astype(jnp.bfloat16)
    grad_queries = contract("bhqk,bkhe->bqhe", score_low, key_low) * score_scale
    grad_keys = contract("bhqk,bqhe->bkhe", score_low, query_low) * score_scale
    grad_queries = grad_queries.reshape(flat_rows, D)
    grad_keys = grad_keys.reshape(flat_rows, D)
    grad_values = grad_values.reshape(flat_rows, D)
    mixed_low = jnp.concatenate([grad_queries, grad_keys, grad_values], axis=1).astype(jnp.bfloat16)
    grad_qkv = matmul_tn(normed1, mixed_low)
    grad_normed1 = matmul_nt(mixed_low, qkv_weight)
    grad_input = grad_residual + normalize_back(grad_normed1, scaled1, inverse1, first_gain)
    head_rows = jnp.stack(
        [
            jnp.sum(grad_normed1 * scaled1, axis=0),
            jnp.sum(grad_normed1, axis=0),
            jnp.sum(grad_queries, axis=0),
            jnp.sum(grad_values, axis=0),
            jnp.sum(grad_residual, axis=0),
            jnp.sum(grad_normed2 * scaled2, axis=0),
            jnp.sum(grad_normed2, axis=0),
        ]
    )
    grad_vectors = jnp.concatenate(
        [
            head_rows,
            jnp.sum(grad_pre, axis=0).reshape(FF // D, D),
            jnp.sum(upstream, axis=0)[None, :],
        ],
        axis=0,
    )
    grads = (grad_qkv, grad_out, grad_up, grad_down, grad_vectors)
    return (
        output.reshape(batch_size, row_count, D),
        grad_input.reshape(batch_size, row_count, D),
        grads,
    )


def local_pieces(flat_slice, share):
    vec_rows = 8 + FF // D
    widths = [share * 3 * D, share * D, share * FF, share * FF, vec_rows * share]
    pieces = []
    offset = 0
    for extent in widths:
        pieces.append(lax.slice_in_dim(flat_slice, offset, offset + extent))
        offset = offset + extent
    return (
        pieces[0].reshape(share, 3 * D),
        pieces[1].reshape(share, D),
        pieces[2].reshape(share, FF),
        pieces[3].reshape(share * FF // D, D),
        pieces[4].reshape(vec_rows, share),
    )


def adam(params, first_moment, second_moment, owned, share):
    local_index = jnp.arange(owned.shape[0], dtype=jnp.int32)
    matrix_mask = (local_index < share * (4 * D + 2 * FF)).astype(jnp.float32)
    new_first = beta_first * first_moment + (1.0 - beta_first) * owned
    new_second = beta_second * second_moment + (1.0 - beta_second) * owned * owned
    fix_first = 1.0 - beta_first**STEP
    fix_second = 1.0 - beta_second**STEP
    ratio = new_first / fix_first / (jnp.sqrt(new_second / fix_second) + adam_eps)
    new_params = params - learn_rate * (ratio + decay_rate * matrix_mask * params)
    return (new_params, new_first, new_second)


def body(x_in, cotangent, params, first_moment, second_moment, seq_lengths, seq_device):
    devices = lax.axis_size("dp") * lax.axis_size("shard")
    share = D // devices
    params_low = params.astype(jnp.bfloat16)
    qkv_part, out_part, up_part, down_part, vec_part = local_pieces(params_low, share)
    weights = (
        lax.all_gather(qkv_part, ("dp", "shard"), axis=0, tiled=True),
        lax.all_gather(out_part, ("dp", "shard"), axis=0, tiled=True),
        lax.all_gather(up_part, ("dp", "shard"), axis=0, tiled=True),
        lax.all_gather(down_part, ("dp", "shard"), axis=0, tiled=True),
        lax.all_gather(vec_part, ("dp", "shard"), axis=1, tiled=True),
    )
    device = lax.axis_index(("dp", "shard"))
    device_ids = jnp.reshape(device, (1,))
    seg_ids, live_mask = segments(seq_lengths, seq_device, device_ids, x_in.shape[0])
    output, grad_input, grads = layer(
        x_in[None], cotangent[None], seg_ids, live_mask, tuple(weights)
    )
    owned_parts = (
        lax.psum_scatter(grads[0], ("dp", "shard"), scatter_dimension=0, tiled=True),
        lax.psum_scatter(grads[1], ("dp", "shard"), scatter_dimension=0, tiled=True),
        lax.psum_scatter(grads[2], ("dp", "shard"), scatter_dimension=0, tiled=True),
        lax.psum_scatter(grads[3], ("dp", "shard"), scatter_dimension=0, tiled=True),
        lax.psum_scatter(grads[4], ("dp", "shard"), scatter_dimension=1, tiled=True),
    )
    owned = jnp.concatenate([piece.reshape(-1) for piece in owned_parts])
    new_params, new_first, new_second = adam(params, first_moment, second_moment, owned, share)
    return (output[0], grad_input[0], owned, new_params, new_first, new_second)

SWAP = ((0, 1), (1, 0))
TEAM = ("x", "c")


def swap(values, axis):
    return lax.ppermute(values, axis, SWAP)


def team_gather(own):
    pair = jnp.stack([own, swap(own, "x")])
    other = swap(pair, "c")
    return jnp.stack([pair, other], axis=1).reshape((4 * own.shape[0],) + own.shape[1:])


def team_reduce(partial):
    blocks = partial.reshape(2, 2, partial.shape[0] // 4, partial.shape[1])
    summed = blocks[:, 0] + swap(blocks[:, 1], "c")
    return summed[0] + swap(summed[1].astype(jnp.bfloat16), "x").astype(jnp.float32)


def both(own, axis_pos):
    other = swap(own, "y")
    return jnp.where(axis_pos == 0, jnp.stack([own, other]), jnp.stack([other, own]))


def y_reduce(blocks, axis_pos):
    mine = lax.dynamic_index_in_dim(blocks, axis_pos, 0, keepdims=False)
    theirs = lax.dynamic_index_in_dim(blocks, 1 - axis_pos, 0, keepdims=False)
    return (mine + swap(theirs.astype(jnp.bfloat16), "y").astype(jnp.float32)).astype(jnp.bfloat16)


def z_gather(shard):
    return lax.all_gather(shard, "z", axis=0, tiled=True)


def z_reduce(values):
    return lax.psum_scatter(values, "z", scatter_dimension=0, tiled=True)


def team_exchange(values):
    return lax.all_to_all(values, TEAM, 0, 0, tiled=True)


def attention(query_low, key_low, value_low, allowed):
    scores = jnp.where(
        allowed, contract("bqhe,bkhe->bhqk", query_low, key_low) * score_scale, neg_large
    )
    row_max = jnp.max(scores, axis=-1, keepdims=True)
    exp_scores = jnp.exp(scores - row_max)
    row_total = jnp.sum(exp_scores, axis=-1, keepdims=True)
    probability = exp_scores / row_total
    log_total = row_max + jnp.log(row_total)
    attended = contract("bhqk,bkhe->bqhe", probability.astype(jnp.bfloat16), value_low)
    return (attended.astype(jnp.bfloat16), log_total)


def attention_back(query_low, key_low, value_low, allowed, log_total, grad_attended):
    scores = jnp.where(
        allowed, contract("bqhe,bkhe->bhqk", query_low, key_low) * score_scale, neg_large
    )
    probability = jnp.where(allowed, jnp.exp(scores - log_total), 0.0)
    grad_prob = contract("bqhe,bkhe->bhqk", grad_attended, value_low)
    grad_values = contract("bhqk,bqhe->bkhe", probability.astype(jnp.bfloat16), grad_attended)
    row_dot = jnp.sum(probability * grad_prob, axis=-1, keepdims=True)
    score_low = (probability * (grad_prob - row_dot)).astype(jnp.bfloat16)
    grad_queries = contract("bhqk,bkhe->bqhe", score_low, key_low) * score_scale
    grad_keys = contract("bhqk,bqhe->bkhe", score_low, query_low) * score_scale
    return (grad_queries, grad_keys, grad_values)


def team_body(x_in, cotangent, params, first_moment, second_moment, seq_lengths, seq_device):
    low = jnp.bfloat16
    rows = x_in.shape[0]
    share = D // 32
    vec_rows = 8 + FF // D
    y_pos = lax.axis_index("y")
    x_pos = lax.axis_index("x")
    c_pos = lax.axis_index("c")
    z_pos = lax.axis_index("z")
    team_pos = x_pos * 2 + c_pos

    qkv_part, out_part, up_part, down_part, vec_part = local_pieces(params.astype(low), share)
    qkv_send = qkv_part.reshape(share, 6, 4, 128).transpose(2, 0, 1, 3).reshape(4, share, 768)
    vec_row = jnp.pad(vec_part.reshape(1, 1, vec_rows * share), ((0, 0), (0, 0), (0, 384)))
    qkv_send = jnp.concatenate([qkv_send, jnp.broadcast_to(vec_row, (4, 1, 768))], axis=1)
    qkv_team = team_exchange(qkv_send)
    vec_team = qkv_team[:, share, :384].reshape(2, 768)
    qkv_shard = jnp.concatenate(
        [qkv_team[:, :share].reshape(4 * share, 768), jnp.pad(vec_team, ((0, 14), (0, 0)))], axis=0
    )
    qkv_z = z_gather(qkv_shard)
    out_z = z_gather(out_part)
    up_send = up_part.reshape(share, 2, 4, 512).transpose(2, 0, 1, 3).reshape(4, share, 1024)
    up_z = z_gather(team_exchange(up_send).reshape(4 * share, 1024))
    down_z = z_gather(down_part)

    qkv_all = both(qkv_z.reshape(4, 144, 768), y_pos)
    qkv_weight = (
        qkv_all[:, :, : 4 * share].reshape(2, 4, 4, share, 768).transpose(0, 2, 1, 3, 4).reshape(D, 768)
    )
    vectors = (
        qkv_all[:, :, 4 * share : 4 * share + 2]
        .reshape(2, 4, 4, vec_rows, share)
        .transpose(3, 0, 2, 1, 4)
        .reshape(vec_rows, D)
        .astype(jnp.float32)
    )
    out_weight = both(out_z, y_pos).reshape(256, D)
    up_weight = (
        both(up_z.reshape(4, 4, share, 1024).transpose(1, 0, 2, 3).reshape(512, 1024), y_pos).reshape(D, 1024)
    )
    down_weight = both(down_z, y_pos).reshape(1024, D)

    first_gain, first_shift = vectors[0], vectors[1]
    out_bias, second_gain, second_shift = vectors[4], vectors[5], vectors[6]
    down_bias = vectors[7 + FF // D]
    pick = lambda row: lax.dynamic_index_in_dim(
        row.reshape(2, 4, row.shape[0] // 8), team_pos, 1, keepdims=False
    ).reshape(-1)
    query_bias, value_bias = pick(vectors[2]), pick(vectors[3])
    up_bias = pick(vectors[7 : 7 + FF // D].reshape(FF))

    steps = jnp.arange(2, dtype=jnp.int32)
    team_devices = (
        ((y_pos * 2 + (x_pos ^ steps[:, None])) * 2 + (c_pos ^ steps[None, :])) * 4 + z_pos
    ).reshape(4)
    seg_ids, live_mask = segments(seq_lengths, seq_device, team_devices.astype(jnp.int32), rows)
    position = jnp.arange(rows, dtype=jnp.int32)
    allowed = (seg_ids[:, :, None] == seg_ids[:, None, :]) & (
        position[None, :, None] >= position[None, None, :]
    )
    allowed = allowed[:, None, :, :]

    upstream = cotangent * live_mask[0][:, None].astype(jnp.float32)
    tokens = team_gather(jnp.stack([x_in, upstream.astype(low)], axis=1))
    x_team, up_low = tokens[:, 0], tokens[:, 1]
    normed1, scaled1, inverse1 = normalize(x_team.astype(jnp.float32), first_gain, first_shift)
    normed1 = normed1.astype(low)
    mixed_all = matmul(normed1, qkv_weight)
    head_shape = (4, rows, 4, HEAD_DIM)
    query_low = (mixed_all[:, :256] + query_bias).astype(low).reshape(head_shape)
    key_low = mixed_all[:, 256:512].astype(low).reshape(head_shape)
    value_low = (mixed_all[:, 512:] + value_bias).astype(low).reshape(head_shape)
    attended, log_total = attention(query_low, key_low, value_low, allowed)
    attended = attended.reshape(4 * rows, 256)
    residual = x_in.astype(jnp.float32) + team_reduce(matmul(attended, out_weight)) + out_bias
    normed2, scaled2, inverse2 = normalize(residual, second_gain, second_shift)
    normed2 = team_gather(normed2.astype(low))
    pre_act = matmul(normed2, up_weight) + up_bias
    act_value, act_slope = gelu_parts(pre_act)
    hidden = act_value.astype(low)
    grad_down = matmul_tn(hidden, up_low)
    down_sum = z_reduce(y_reduce(grad_down.reshape(2, 512, D), y_pos))
    grad_pre = matmul_nt(up_low, down_weight) * act_slope
    pre_low = grad_pre.astype(low)
    grad_normed2 = team_reduce(matmul_nt(pre_low, up_weight))
    grad_up = matmul_tn(normed2, pre_low)
    up_sum = z_reduce(
        y_reduce(grad_up.reshape(2, 512, 1024), y_pos)
        .reshape(4, 4, share, 1024)
        .transpose(1, 0, 2, 3)
        .reshape(512, 1024)
    )
    output = residual + team_reduce(matmul(hidden, down_weight)) + down_bias
    grad_residual = upstream + normalize_back(grad_normed2, scaled2, inverse2, second_gain)
    res_low = team_gather(grad_residual.astype(low))
    grad_attended = matmul_nt(res_low, out_weight).astype(low).reshape(head_shape)
    grad_out = matmul_tn(attended, res_low)
    out_sum = z_reduce(y_reduce(grad_out.reshape(2, 128, D), y_pos))
    grad_queries, grad_keys, grad_values = attention_back(
        query_low, key_low, value_low, allowed, log_total, grad_attended
    )
    grad_queries = grad_queries.reshape(4 * rows, 256)
    grad_keys = grad_keys.reshape(4 * rows, 256)
    grad_values = grad_values.reshape(4 * rows, 256)
    mixed_low = jnp.concatenate([grad_queries, grad_keys, grad_values], axis=1).astype(low)
    partial1 = matmul_nt(mixed_low, qkv_weight)
    grad_qkv = matmul_tn(normed1, mixed_low)

    own_team = (jnp.arange(4, dtype=jnp.int32) == team_pos).astype(jnp.float32)[None, :, None]
    place = lambda row: (row.reshape(2, 1, -1) * own_team).reshape(-1)
    grad_vectors = jnp.concatenate(
        [
            jnp.stack(
                [
                    jnp.sum(partial1 * scaled1, axis=0),
                    jnp.sum(partial1, axis=0),
                    place(jnp.sum(grad_queries, axis=0)),
                    place(jnp.sum(grad_values, axis=0)),
                    jnp.sum(grad_residual, axis=0),
                    jnp.sum(grad_normed2 * scaled2, axis=0),
                    jnp.sum(grad_normed2, axis=0),
                ]
            ),
            place(jnp.sum(grad_pre, axis=0)).reshape(FF // D, D),
            jnp.sum(upstream, axis=0)[None, :],
        ],
        axis=0,
    )
    vec_blocks = (
        grad_vectors.reshape(vec_rows, 2, 4, 4, share).transpose(1, 3, 2, 0, 4).reshape(2, 4, 2, 768)
    )
    qkv_blocks = grad_qkv.reshape(2, 4, 4, share, 768).transpose(0, 2, 1, 3, 4).reshape(2, 4, 4 * share, 768)
    qkv_blocks = jnp.concatenate(
        [qkv_blocks, jnp.pad(vec_blocks, ((0, 0), (0, 0), (0, 14), (0, 0)))], axis=2
    )
    qkv_sum = z_reduce(y_reduce(qkv_blocks.reshape(2, 576, 768), y_pos))
    qkv_back = jnp.concatenate(
        [
            qkv_sum[: 4 * share].reshape(4, share, 768),
            jnp.pad(qkv_sum[4 * share : 4 * share + 2].reshape(4, 1, 384), ((0, 0), (0, 0), (0, 384))),
        ],
        axis=1,
    )
    qkv_own = team_exchange(qkv_back).astype(jnp.float32)
    up_own = team_exchange(up_sum.reshape(4, share, 1024)).astype(jnp.float32)

    grad_normed1 = team_reduce(partial1)
    grad_input = grad_residual + normalize_back(
        grad_normed1, scaled1[:rows], inverse1[:rows], first_gain
    )
    owned = jnp.concatenate(
        [
            qkv_own[:, :share].reshape(4, share, 6, 128).transpose(1, 2, 0, 3).reshape(-1),
            out_sum.astype(jnp.float32).reshape(-1),
            up_own.reshape(4, share, 2, 512).transpose(1, 2, 0, 3).reshape(-1),
            down_sum.astype(jnp.float32).reshape(-1),
            jnp.sum(qkv_own[:, share, :384], axis=0),
        ]
    )
    new_params, new_first, new_second = adam(params, first_moment, second_moment, owned, share)
    return (output, grad_input, owned, new_params, new_first, new_second)


def solution(mesh):
    shape = dict(mesh.shape)
    if shape["dp"] == 8 and shape["shard"] == 4:
        mesh = Mesh(mesh.devices.reshape(2, 2, 2, 4), ("y", "x", "c", "z"))
        axes, step = ("y", "x", "c", "z"), team_body
    else:
        axes, step = ("dp", "shard"), body
    return jax.shard_map(
        step,
        mesh=mesh,
        in_specs=(P(axes, None), P(axes, None), P(axes), P(axes), P(axes), P(), P()),
        out_specs=(P(axes, None), P(axes, None), P(axes), P(axes), P(axes), P(axes)),
        check_vma=False,
    )
```

```python
import jax
import jax.numpy as jnp
from jax import lax
from jax.experimental import pallas as pl
from jax.experimental.pallas import tpu as pltpu
from jax.sharding import Mesh
from jax.sharding import PartitionSpec as P

D = 1024
HEADS = 16
HEAD_DIM = 64
FF = 4096
STEP = 4


score_scale = 0.125
norm_eps = 1e-05
gelu_coef = 0.7978845608028654
gelu_cubic = 0.044715
learn_rate = 0.01
beta_first = 0.9
beta_second = 0.95
adam_eps = 1e-08
decay_rate = 0.1
neg_large = -1e30


def matmul(left_side, right_side):
    return jnp.dot(left_side, right_side, preferred_element_type=jnp.float32)


def matmul_tn(left_side, right_side):
    return lax.dot_general(
        left_side, right_side, (((0,), (0,)), ((), ())), preferred_element_type=jnp.float32
    )


def matmul_nt(left_side, right_side):
    return lax.dot_general(
        left_side, right_side, (((1,), (1,)), ((), ())), preferred_element_type=jnp.float32
    )


def contract(pattern, left_side, right_side):
    return jnp.einsum(pattern, left_side, right_side, preferred_element_type=jnp.float32)


def normalize(values, norm_gain, norm_shift):
    average = jnp.mean(values, axis=-1, keepdims=True)
    centered = values - average
    inverse = lax.rsqrt(jnp.mean(centered * centered, axis=-1, keepdims=True) + norm_eps)
    scaled = centered * inverse
    return (scaled * norm_gain + norm_shift, scaled, inverse)


def normalize_back(upstream, scaled, inverse, norm_gain):
    grad_scaled = upstream * norm_gain
    term_one = jnp.mean(grad_scaled, axis=-1, keepdims=True)
    term_two = jnp.mean(grad_scaled * scaled, axis=-1, keepdims=True)
    return inverse * (grad_scaled - term_one - scaled * term_two)


def gelu_parts(pre_act):
    inner_arg = gelu_coef * (pre_act + gelu_cubic * pre_act * pre_act * pre_act)
    tanh_val = jnp.tanh(inner_arg)
    act_value = 0.5 * pre_act * (1.0 + tanh_val)
    act_slope = 0.5 * (1.0 + tanh_val) + 0.5 * pre_act * (1.0 - tanh_val * tanh_val) * gelu_coef * (
        1.0 + 3.0 * gelu_cubic * pre_act * pre_act
    )
    return (act_value, act_slope)


def segments(seq_lengths, seq_device, device_ids, row_count):
    owned = seq_device[None, :] == device_ids[:, None]
    own_lengths = jnp.where(owned, seq_lengths[None, :], 0)
    ends = jnp.cumsum(own_lengths, axis=1)
    position = jnp.arange(row_count, dtype=jnp.int32)
    passed = owned[:, None, :] & (ends[:, None, :] <= position[None, :, None])
    seg_ids = jnp.sum(passed.astype(jnp.int32), axis=2)
    live_mask = position[None, :] < ends[:, -1:]
    return (seg_ids, live_mask)


def layer(x_in, cotangent, seg_ids, live_mask, weights):
    qkv_weight, out_weight, up_weight, down_weight, vectors = weights
    vectors = vectors.astype(jnp.float32)
    first_gain = vectors[0]
    first_shift = vectors[1]
    query_bias = vectors[2]
    value_bias = vectors[3]
    out_bias = vectors[4]
    second_gain = vectors[5]
    second_shift = vectors[6]
    up_bias = vectors[7 : 7 + FF // D].reshape(FF)
    down_bias = vectors[7 + FF // D]
    batch_size = x_in.shape[0]
    row_count = x_in.shape[1]
    flat_rows = batch_size * row_count
    head_shape = (batch_size, row_count, HEADS, HEAD_DIM)
    stream = x_in.astype(jnp.float32).reshape(flat_rows, D)
    normed1, scaled1, inverse1 = normalize(stream, first_gain, first_shift)
    normed1 = normed1.astype(jnp.bfloat16)
    mixed_all = matmul(normed1, qkv_weight)
    query_low = (mixed_all[:, :D] + query_bias).astype(jnp.bfloat16).reshape(head_shape)
    key_low = mixed_all[:, D : 2 * D].astype(jnp.bfloat16).reshape(head_shape)
    value_low = (mixed_all[:, 2 * D :] + value_bias).astype(jnp.bfloat16).reshape(head_shape)
    position = jnp.arange(row_count, dtype=jnp.int32)
    allowed = (seg_ids[:, :, None] == seg_ids[:, None, :]) & (
        position[None, :, None] >= position[None, None, :]
    )
    allowed = allowed[:, None, :, :]
    scores = jnp.where(
        allowed, contract("bqhe,bkhe->bhqk", query_low, key_low) * score_scale, neg_large
    )
    row_max = jnp.max(scores, axis=-1, keepdims=True)
    exp_scores = jnp.exp(scores - row_max)
    row_total = jnp.sum(exp_scores, axis=-1, keepdims=True)
    probability = exp_scores / row_total
    log_total = row_max + jnp.log(row_total)
    attended = contract("bhqk,bkhe->bqhe", probability.astype(jnp.bfloat16), value_low)
    attended = attended.astype(jnp.bfloat16).reshape(flat_rows, D)
    residual = stream + matmul(attended, out_weight) + out_bias
    normed2, scaled2, inverse2 = normalize(residual, second_gain, second_shift)
    normed2 = normed2.astype(jnp.bfloat16)
    pre_act = matmul(normed2, up_weight) + up_bias
    act_value, act_slope = gelu_parts(pre_act)
    hidden = act_value.astype(jnp.bfloat16)
    output = residual + matmul(hidden, down_weight) + down_bias
    upstream = cotangent.reshape(flat_rows, D) * live_mask.reshape(flat_rows, 1).astype(jnp.float32)
    up_low = upstream.astype(jnp.bfloat16)
    grad_down = matmul_tn(hidden, up_low)
    grad_pre = matmul_nt(up_low, down_weight) * act_slope
    pre_low = grad_pre.astype(jnp.bfloat16)
    grad_up = matmul_tn(normed2, pre_low)
    grad_normed2 = matmul_nt(pre_low, up_weight)
    grad_residual = upstream + normalize_back(grad_normed2, scaled2, inverse2, second_gain)
    res_low = grad_residual.astype(jnp.bfloat16)
    grad_out = matmul_tn(attended, res_low)
    grad_attended = matmul_nt(res_low, out_weight).astype(jnp.bfloat16).reshape(head_shape)
    scores = jnp.where(
        allowed, contract("bqhe,bkhe->bhqk", query_low, key_low) * score_scale, neg_large
    )
    probability = jnp.where(allowed, jnp.exp(scores - log_total), 0.0)
    grad_prob = contract("bqhe,bkhe->bhqk", grad_attended, value_low)
    grad_values = contract("bhqk,bqhe->bkhe", probability.astype(jnp.bfloat16), grad_attended)
    row_dot = jnp.sum(probability * grad_prob, axis=-1, keepdims=True)
    score_low = (probability * (grad_prob - row_dot)).astype(jnp.bfloat16)
    grad_queries = contract("bhqk,bkhe->bqhe", score_low, key_low) * score_scale
    grad_keys = contract("bhqk,bqhe->bkhe", score_low, query_low) * score_scale
    grad_queries = grad_queries.reshape(flat_rows, D)
    grad_keys = grad_keys.reshape(flat_rows, D)
    grad_values = grad_values.reshape(flat_rows, D)
    mixed_low = jnp.concatenate([grad_queries, grad_keys, grad_values], axis=1).astype(jnp.bfloat16)
    grad_qkv = matmul_tn(normed1, mixed_low)
    grad_normed1 = matmul_nt(mixed_low, qkv_weight)
    grad_input = grad_residual + normalize_back(grad_normed1, scaled1, inverse1, first_gain)
    head_rows = jnp.stack(
        [
            jnp.sum(grad_normed1 * scaled1, axis=0),
            jnp.sum(grad_normed1, axis=0),
            jnp.sum(grad_queries, axis=0),
            jnp.sum(grad_values, axis=0),
            jnp.sum(grad_residual, axis=0),
            jnp.sum(grad_normed2 * scaled2, axis=0),
            jnp.sum(grad_normed2, axis=0),
        ]
    )
    grad_vectors = jnp.concatenate(
        [
            head_rows,
            jnp.sum(grad_pre, axis=0).reshape(FF // D, D),
            jnp.sum(upstream, axis=0)[None, :],
        ],
        axis=0,
    )
    grads = (grad_qkv, grad_out, grad_up, grad_down, grad_vectors)
    return (
        output.reshape(batch_size, row_count, D),
        grad_input.reshape(batch_size, row_count, D),
        grads,
    )


def local_pieces(flat_slice, share):
    vec_rows = 8 + FF // D
    widths = [share * 3 * D, share * D, share * FF, share * FF, vec_rows * share]
    pieces = []
    offset = 0
    for extent in widths:
        pieces.append(lax.slice_in_dim(flat_slice, offset, offset + extent))
        offset = offset + extent
    return (
        pieces[0].reshape(share, 3 * D),
        pieces[1].reshape(share, D),
        pieces[2].reshape(share, FF),
        pieces[3].reshape(share * FF // D, D),
        pieces[4].reshape(vec_rows, share),
    )


def adam(params, first_moment, second_moment, owned, share):
    local_index = jnp.arange(owned.shape[0], dtype=jnp.int32)
    matrix_mask = (local_index < share * (4 * D + 2 * FF)).astype(jnp.float32)
    new_first = beta_first * first_moment + (1.0 - beta_first) * owned
    new_second = beta_second * second_moment + (1.0 - beta_second) * owned * owned
    fix_first = 1.0 - beta_first**STEP
    fix_second = 1.0 - beta_second**STEP
    ratio = new_first / fix_first / (jnp.sqrt(new_second / fix_second) + adam_eps)
    new_params = params - learn_rate * (ratio + decay_rate * matrix_mask * params)
    return (new_params, new_first, new_second)


def body(x_in, cotangent, params, first_moment, second_moment, seq_lengths, seq_device):
    devices = lax.axis_size("dp") * lax.axis_size("shard")
    share = D // devices
    params_low = params.astype(jnp.bfloat16)
    qkv_part, out_part, up_part, down_part, vec_part = local_pieces(params_low, share)
    weights = (
        lax.all_gather(qkv_part, ("dp", "shard"), axis=0, tiled=True),
        lax.all_gather(out_part, ("dp", "shard"), axis=0, tiled=True),
        lax.all_gather(up_part, ("dp", "shard"), axis=0, tiled=True),
        lax.all_gather(down_part, ("dp", "shard"), axis=0, tiled=True),
        lax.all_gather(vec_part, ("dp", "shard"), axis=1, tiled=True),
    )
    device = lax.axis_index(("dp", "shard"))
    device_ids = jnp.reshape(device, (1,))
    seg_ids, live_mask = segments(seq_lengths, seq_device, device_ids, x_in.shape[0])
    output, grad_input, grads = layer(
        x_in[None], cotangent[None], seg_ids, live_mask, tuple(weights)
    )
    owned_parts = (
        lax.psum_scatter(grads[0], ("dp", "shard"), scatter_dimension=0, tiled=True),
        lax.psum_scatter(grads[1], ("dp", "shard"), scatter_dimension=0, tiled=True),
        lax.psum_scatter(grads[2], ("dp", "shard"), scatter_dimension=0, tiled=True),
        lax.psum_scatter(grads[3], ("dp", "shard"), scatter_dimension=0, tiled=True),
        lax.psum_scatter(grads[4], ("dp", "shard"), scatter_dimension=1, tiled=True),
    )
    owned = jnp.concatenate([piece.reshape(-1) for piece in owned_parts])
    new_params, new_first, new_second = adam(params, first_moment, second_moment, owned, share)
    return (output[0], grad_input[0], owned, new_params, new_first, new_second)

SWAP = ((0, 1), (1, 0))
TEAM = ("x", "c")
LOW = jnp.bfloat16
TOK = 512
ROW = 128


def swap(values, axis):
    return lax.ppermute(values, axis, SWAP)


def z_gather(shard):
    return lax.all_gather(shard, "z", axis=0, tiled=True)


def z_reduce(values):
    return lax.psum_scatter(values, "z", scatter_dimension=0, tiled=True)


def team_exchange(values):
    return lax.all_to_all(values, TEAM, 0, 0, tiled=True)


def team_gather(own):
    near = swap(own, "x")
    return (own, near, swap(own, "c"), swap(near, "c"))


def team_reduce(keep, send):
    summed = keep + swap(send, "c")
    return (summed[:ROW], swap(summed[ROW:].astype(LOW), "x"))


def sds(shape, dtype=jnp.float32):
    return jax.ShapeDtypeStruct(shape, dtype)


def call(kernel, name, outs, operands, scratch=()):
    specs = [pl.BlockSpec(memory_space=pltpu.SMEM)] + [
        pl.BlockSpec(memory_space=pltpu.VMEM) for _ in operands[1:]
    ]
    return pl.pallas_call(
        kernel,
        out_shape=outs,
        in_specs=specs,
        out_specs=tuple(pl.BlockSpec(memory_space=pltpu.VMEM) for _ in outs),
        scratch_shapes=scratch,
        name=name,
        compiler_params=pltpu.CompilerParams(vmem_limit_bytes=48 << 20),
    )(*operands)


def head_lanes():
    return lax.broadcasted_iota(jnp.int32, (ROW, 128), 1) < HEAD_DIM


def lane_group(rows):
    return lax.broadcasted_iota(jnp.int32, (rows, 128), 1) // 32


def allowed_block(seg_col, seg_row, block):
    query_at = lax.broadcasted_iota(jnp.int32, (ROW, ROW), 0)
    key_at = lax.broadcasted_iota(jnp.int32, (ROW, ROW), 1)
    return (seg_col[block * ROW : (block + 1) * ROW, :] == seg_row[block : block + 1, :]) & (
        query_at >= key_at
    )


def scores_of(query_low, key_low, allowed):
    return jnp.where(allowed, matmul_nt(query_low, key_low) * score_scale, neg_large)


def forward_kernel(
    at, x_ref, own_ref, far_ref, out_own, out_far, seg_col, seg_row,
    vec_ref, weight_ref, out_ref, normed_ref, qkv_ref, att_ref, keep_ref, send_ref,
):
    y_pos, team = at[0], at[1]
    group = lane_group(16)
    for ref, out_part, side in ((own_ref, out_own, y_pos), (far_ref, out_far, 1 - y_pos)):
        base = side * 512
        for z in range(4):
            for t in range(4):
                start = pl.multiple_of(base + t * 128 + z * 32, 32)
                weight_ref[pl.ds(start, 32), :] = ref[z, t * 32 : (t + 1) * 32, :]
        for t in range(4):
            tile = jnp.zeros((16, 128), jnp.float32)
            for z in range(4):
                piece = ref[z, 128:144, 0:128].astype(jnp.float32)
                shift = (z - t) * 32 % 128
                piece = pltpu.roll(piece, shift, 1) if shift else piece
                tile = jnp.where(group == z, piece, tile)
            vec_ref[:, pl.ds(pl.multiple_of(base + t * 128, 128), 128)] = tile
        out_ref[pl.ds(pl.multiple_of(side * 128, 128), 128), :] = out_part[...]
    gain, shift_row = vec_ref[0:1, :], vec_ref[1:2, :]
    for block in range(4):
        rows = slice(block * ROW, (block + 1) * ROW)
        value, _, _ = normalize(x_ref[rows, :].astype(jnp.float32), gain, shift_row)
        normed_ref[rows, :] = value.astype(LOW)
    for block in range(4):
        rows = slice(block * ROW, (block + 1) * ROW)
        mixed = matmul(normed_ref[rows, :], weight_ref[...])
        for pair in range(2):
            lanes = pl.ds(pl.multiple_of(pair * 512 + team * 128, 128), 128)
            for which in range(3):
                cols = slice(which * 256 + pair * 128, which * 256 + (pair + 1) * 128)
                piece = mixed[:, cols]
                if which == 0:
                    piece = piece + vec_ref[2:3, lanes]
                if which == 2:
                    piece = piece + vec_ref[3:4, lanes]
                qkv_ref[rows, cols] = piece.astype(LOW)
    first = head_lanes()
    for block in range(4):
        rows = slice(block * ROW, (block + 1) * ROW)
        allowed = allowed_block(seg_col, seg_row, block)
        for pair in range(2):
            query, key, value = (
                qkv_ref[rows, w * 256 + pair * 128 : w * 256 + (pair + 1) * 128] for w in range(3)
            )
            heads = []
            for mask in (first, ~first):
                scores = scores_of(jnp.where(mask, query, jnp.zeros_like(query)), key, allowed)
                row_max = jnp.max(scores, axis=-1, keepdims=True)
                exp_scores = jnp.exp(scores - row_max)
                row_total = jnp.sum(exp_scores, axis=-1, keepdims=True)
                heads.append(matmul((exp_scores / row_total).astype(LOW), value))
            att_ref[rows, pair * 128 : (pair + 1) * 128] = jnp.where(first, heads[0], heads[1]).astype(LOW)
    keep_ref[...] = matmul(att_ref[0:256, :], out_ref[...])
    send_ref[...] = matmul(att_ref[256:512, :], out_ref[...])


def residual_kernel(at, x_ref, sum_ref, near_ref, vec_ref, res_ref, low_ref):
    total = sum_ref[...] + near_ref[...].astype(jnp.float32)
    residual = x_ref[...].astype(jnp.float32) + total + vec_ref[4:5, :]
    res_ref[...] = residual
    value, _, _ = normalize(residual, vec_ref[5:6, :], vec_ref[6:7, :])
    low_ref[...] = value.astype(LOW)


def up_kernel(
    at, n0, n1, n2, n3, own_ref, far_ref, bias_ref, uplow_ref,
    team_ref, weight_ref, hidden_ref, slope_ref, mine_ref, theirs_ref, grad_ref,
):
    y_pos = at[0]
    for block, ref in enumerate((n0, n1, n2, n3)):
        team_ref[block * ROW : (block + 1) * ROW, :] = ref[...]
    for ref, side in ((own_ref, y_pos), (far_ref, 1 - y_pos)):
        for z in range(4):
            for t in range(4):
                start = pl.multiple_of(side * 512 + t * 128 + z * 32, 32)
                weight_ref[pl.ds(start, 32), :] = ref[z, t * 32 : (t + 1) * 32, :]
    for block in range(4):
        rows = slice(block * ROW, (block + 1) * ROW)
        pre_act = matmul(team_ref[rows, :], weight_ref[...]) + bias_ref[...]
        act_value, act_slope = gelu_parts(pre_act)
        hidden_ref[rows, :] = act_value.astype(LOW)
        slope_ref[rows, :] = act_slope
    grad_ref[...] = matmul_tn(hidden_ref[...], uplow_ref[...])
    mine_ref[...] = grad_ref[pl.ds(pl.multiple_of(y_pos * 512, 512), 512), :]
    theirs_ref[...] = grad_ref[pl.ds(pl.multiple_of((1 - y_pos) * 512, 512), 512), :].astype(LOW)


def down_kernel(
    at, uplow_ref, own_ref, far_ref, slope_ref, weight_ref,
    pre_ref, sum_ref, keep_ref, send_ref,
):
    y_pos = at[0]
    sum_ref[...] = jnp.zeros_like(sum_ref)
    for ref, side in ((own_ref, y_pos), (far_ref, 1 - y_pos)):
        cols = pl.ds(pl.multiple_of(side * 512, 512), 512)
        for block in range(4):
            rows = slice(block * ROW, (block + 1) * ROW)
            grad_pre = matmul_nt(uplow_ref[rows, :], ref[...]) * slope_ref[rows, cols]
            pre_ref[rows, cols] = grad_pre.astype(LOW)
            sum_ref[0:1, cols] += jnp.sum(grad_pre, axis=0, keepdims=True)
    keep_ref[...] = matmul_nt(pre_ref[0:256, :], weight_ref[...])
    send_ref[...] = matmul_nt(pre_ref[256:512, :], weight_ref[...])


def spread(at, grad_ref, mine_ref, theirs_ref):
    y_pos = at[0]
    for z in range(4):
        for t in range(4):
            near = pl.multiple_of(y_pos * 512 + t * 128 + z * 32, 32)
            away = pl.multiple_of((1 - y_pos) * 512 + t * 128 + z * 32, 32)
            mine_ref[z, t * 32 : (t + 1) * 32, :] = grad_ref[pl.ds(near, 32), :]
            theirs_ref[z, t * 32 : (t + 1) * 32, :] = grad_ref[pl.ds(away, 32), :].astype(LOW)


def up_grad_kernel(at, team_ref, pre_ref, mine_ref, theirs_ref, grad_ref):
    grad_ref[...] = matmul_tn(team_ref[...], pre_ref[...])
    spread(at, grad_ref, mine_ref, theirs_ref)


def output_kernel(at, hidden_ref, own_ref, far_ref, keep_ref, send_ref):
    y_pos = at[0]
    near = pl.ds(pl.multiple_of(y_pos * 512, 512), 512)
    away = pl.ds(pl.multiple_of((1 - y_pos) * 512, 512), 512)
    for ref, base in ((keep_ref, 0), (send_ref, 256)):
        rows = slice(base, base + 256)
        ref[...] = matmul(hidden_ref[rows, near], own_ref[...]) + matmul(hidden_ref[rows, away], far_ref[...])


def residual_back_kernel(
    at, res_ref, sum_ref, near_ref, up_ref, vec_ref, grad_ref, low_ref, rows_ref
):
    _, scaled, inverse = normalize(res_ref[...], vec_ref[5:6, :], vec_ref[6:7, :])
    grad_normed = sum_ref[...] + near_ref[...].astype(jnp.float32)
    upstream = up_ref[...]
    grad = upstream + normalize_back(grad_normed, scaled, inverse, vec_ref[5:6, :])
    grad_ref[...] = grad
    low_ref[...] = grad.astype(LOW)
    total = lambda value: jnp.sum(value, axis=0, keepdims=True)
    rows_ref[...] = jnp.zeros_like(rows_ref)
    rows_ref[0:1, :] = total(grad)
    rows_ref[1:2, :] = total(grad_normed * scaled)
    rows_ref[2:3, :] = total(grad_normed)
    rows_ref[3:4, :] = total(upstream)


def out_grad_kernel(at, r0, r1, r2, r3, att_ref, team_ref, mine_ref, theirs_ref, grad_ref):
    y_pos = at[0]
    for block, ref in enumerate((r0, r1, r2, r3)):
        team_ref[block * ROW : (block + 1) * ROW, :] = ref[...]
    grad_ref[...] = matmul_tn(att_ref[...], team_ref[...])
    mine_ref[...] = grad_ref[pl.ds(pl.multiple_of(y_pos * 128, 128), 128), :]
    theirs_ref[...] = grad_ref[pl.ds(pl.multiple_of((1 - y_pos) * 128, 128), 128), :].astype(LOW)


def backward_kernel(
    at, team_ref, out_ref, qkv_ref, normed_ref, x_ref, weight_ref, seg_col, seg_row, rows_ref,
    mine_ref, theirs_ref, keep_ref, send_ref,
    mixed_ref, grad_ref, att_ref, vec_ref,
):
    y_pos, team = at[0], at[1]
    att_ref[...] = matmul_nt(team_ref[...], out_ref[...]).astype(LOW)
    vec_ref[...] = rows_ref[...]
    first = head_lanes()
    for pair in range(2):
        query_sum = jnp.zeros((1, 128), jnp.float32)
        value_sum = jnp.zeros((1, 128), jnp.float32)
        for block in range(4):
            rows = slice(block * ROW, (block + 1) * ROW)
            allowed = allowed_block(seg_col, seg_row, block)
            query, key, value = (
                qkv_ref[rows, w * 256 + pair * 128 : w * 256 + (pair + 1) * 128] for w in range(3)
            )
            grad_att = att_ref[rows, pair * 128 : (pair + 1) * 128]
            parts = []
            for mask in (first, ~first):
                scores = scores_of(jnp.where(mask, query, jnp.zeros_like(query)), key, allowed)
                row_max = jnp.max(scores, axis=-1, keepdims=True)
                log_total = row_max + jnp.log(jnp.sum(jnp.exp(scores - row_max), axis=-1, keepdims=True))
                probability = jnp.where(allowed, jnp.exp(scores - log_total), 0.0)
                grad_prob = matmul_nt(jnp.where(mask, grad_att, jnp.zeros_like(grad_att)), value)
                grad_value = matmul_tn(probability.astype(LOW), grad_att)
                row_dot = jnp.sum(probability * grad_prob, axis=-1, keepdims=True)
                score_low = (probability * (grad_prob - row_dot)).astype(LOW)
                parts.append(
                    (matmul(score_low, key) * score_scale, matmul_tn(score_low, query) * score_scale, grad_value)
                )
            for which in range(3):
                merged = jnp.where(first, parts[0][which], parts[1][which])
                mixed_ref[rows, which * 256 + pair * 128 : which * 256 + (pair + 1) * 128] = merged.astype(LOW)
                if which == 0:
                    query_sum = query_sum + jnp.sum(merged, axis=0, keepdims=True)
                if which == 2:
                    value_sum = value_sum + jnp.sum(merged, axis=0, keepdims=True)
        lanes = pl.ds(pl.multiple_of(pair * 512 + team * 128, 128), 128)
        vec_ref[2:3, lanes] = query_sum
        vec_ref[3:4, lanes] = value_sum
    grad_ref[...] = matmul_tn(normed_ref[...], mixed_ref[...])
    spread(at, grad_ref, mine_ref, theirs_ref)
    keep_ref[...] = matmul_nt(mixed_ref[0:256, :], weight_ref[...])
    send_ref[...] = matmul_nt(mixed_ref[256:512, :], weight_ref[...])
    gain_sum = jnp.zeros((1, D), jnp.float32)
    shift_sum = jnp.zeros((1, D), jnp.float32)
    for block in range(4):
        rows = slice(block * ROW, (block + 1) * ROW)
        _, scaled, _ = normalize(x_ref[rows, :].astype(jnp.float32), 1.0, 0.0)
        source, at_row = (keep_ref, block) if block < 2 else (send_ref, block - 2)
        partial = source[at_row * ROW : (at_row + 1) * ROW, :]
        gain_sum = gain_sum + jnp.sum(partial * scaled, axis=0, keepdims=True)
        shift_sum = shift_sum + jnp.sum(partial, axis=0, keepdims=True)
    vec_ref[0:1, :] = gain_sum
    vec_ref[1:2, :] = shift_sum
    group = lane_group(16)
    for ref, side, kind in ((mine_ref, y_pos, jnp.float32), (theirs_ref, 1 - y_pos, LOW)):
        for z in range(4):
            tile = jnp.zeros((16, 128), jnp.float32)
            for t in range(4):
                piece = vec_ref[:, pl.ds(pl.multiple_of(side * 512 + t * 128, 128), 128)]
                shift = (t - z) * 32 % 128
                piece = pltpu.roll(piece, shift, 1) if shift else piece
                tile = jnp.where(group == t, piece, tile)
            ref[z, 128:144, 0:128] = tile.astype(kind)
            ref[z, 128:144, 128:768] = jnp.zeros((16, 640), kind)


def team_body(x_in, cotangent, params, first_moment, second_moment, seq_lengths, seq_device):
    rows = x_in.shape[0]
    share = D // 32
    vec_rows = 8 + FF // D
    y_pos = lax.axis_index("y")
    x_pos = lax.axis_index("x")
    c_pos = lax.axis_index("c")
    z_pos = lax.axis_index("z")
    team_pos = x_pos * 2 + c_pos
    at = jnp.stack([y_pos, team_pos]).astype(jnp.int32)

    qkv_part, out_part, up_part, down_part, vec_part = local_pieces(params.astype(LOW), share)
    qkv_send = qkv_part.reshape(share, 6, 4, 128).transpose(2, 0, 1, 3).reshape(4, share, 768)
    vec_row = jnp.broadcast_to(jnp.pad(vec_part, ((0, 4), (0, 736)))[None], (4, 16, 768))
    qkv_team = team_exchange(jnp.concatenate([qkv_send, vec_row], axis=1))
    vec_team = qkv_team[:, share:, :32].transpose(1, 0, 2).reshape(16, 128)
    qkv_shard = jnp.concatenate(
        [qkv_team[:, :share].reshape(4 * share, 768), jnp.pad(vec_team, ((0, 0), (0, 640)))], axis=0
    )
    qkv_own = z_gather(qkv_shard).reshape(4, 144, 768)
    out_own = z_gather(out_part)
    up_send = up_part.reshape(share, 2, 4, 512).transpose(2, 0, 1, 3).reshape(4, share, 1024)
    up_own = z_gather(team_exchange(up_send).reshape(4 * share, 1024)).reshape(4, 4 * share, 1024)
    down_own = z_gather(down_part)
    qkv_far, out_far, up_far, down_far = (swap(v, "y") for v in (qkv_own, out_own, up_own, down_own))

    steps = jnp.arange(2, dtype=jnp.int32)
    team_devices = (
        ((y_pos * 2 + (x_pos ^ steps[None, :])) * 2 + (c_pos ^ steps[:, None])) * 4 + z_pos
    ).reshape(4)
    seg_ids, live_mask = segments(seq_lengths, seq_device, team_devices.astype(jnp.int32), rows)
    seg_col = seg_ids.reshape(4 * rows, 1)

    upstream = cotangent * live_mask[0][:, None].astype(jnp.float32)
    tokens = jnp.stack(team_gather(jnp.stack([x_in, upstream.astype(LOW)])))
    x_team = tokens[:, 0].reshape(TOK, D)
    up_low = tokens[:, 1].reshape(TOK, D)

    vectors, qkv_weight, out_weight, normed1, qkv_low, attended, keep, send = call(
        forward_kernel,
        "attention_forward",
        (
            sds((16, D)), sds((D, 768), LOW), sds((256, D), LOW), sds((TOK, D), LOW),
            sds((TOK, 768), LOW), sds((TOK, 256), LOW), sds((256, D)), sds((256, D)),
        ),
        (at, x_team, qkv_own, qkv_far, out_own, out_far, seg_col, seg_ids),
    )
    up_bias = lax.dynamic_index_in_dim(
        vectors[7 : 7 + FF // D].reshape(2, 4, 512), team_pos, 1, keepdims=False
    ).reshape(1, 1024)
    summed, near = team_reduce(keep, send)
    residual, normed2 = call(
        residual_kernel, "residual", (sds((rows, D)), sds((rows, D), LOW)), (at, x_in, summed, near, vectors)
    )
    normed2, up_weight, hidden, slope, down_mine, down_theirs = call(
        up_kernel,
        "up_forward",
        (
            sds((TOK, D), LOW), sds((D, 1024), LOW), sds((TOK, 1024), LOW), sds((TOK, 1024)),
            sds((512, D)), sds((512, D), LOW),
        ),
        (at, *team_gather(normed2), up_own, up_far, up_bias, up_low),
        [pltpu.VMEM((1024, D), jnp.float32)],
    )
    y_sum = lambda mine, theirs: (mine + swap(theirs, "y").astype(jnp.float32)).astype(LOW)
    down_sum = z_reduce(y_sum(down_mine, down_theirs))
    pre_low, pre_sum, keep, send = call(
        down_kernel,
        "down_backward",
        (sds((TOK, 1024), LOW), sds((8, 1024)), sds((256, D)), sds((256, D))),
        (at, up_low, down_own, down_far, slope, up_weight),
    )
    summed, near = team_reduce(keep, send)
    grad_residual, res_low, row_sums = call(
        residual_back_kernel,
        "residual_backward",
        (sds((rows, D)), sds((rows, D), LOW), sds((8, D))),
        (at, residual, summed, near, upstream, vectors),
    )
    up_mine, up_theirs = call(
        up_grad_kernel,
        "up_grad",
        (sds((4, 4 * share, 1024)), sds((4, 4 * share, 1024), LOW)),
        (at, normed2, pre_low),
        [pltpu.VMEM((D, 1024), jnp.float32)],
    )
    up_sum = z_reduce(y_sum(up_mine, up_theirs).reshape(TOK, 1024))
    keep, send = call(
        output_kernel, "down_forward", (sds((256, D)), sds((256, D))), (at, hidden, down_own, down_far)
    )
    summed, near = team_reduce(keep, send)
    output = residual + summed + near.astype(jnp.float32) + vectors[7 + FF // D]
    res_team, out_mine, out_theirs = call(
        out_grad_kernel,
        "out_grad",
        (sds((TOK, D), LOW), sds((128, D)), sds((128, D), LOW)),
        (at, *team_gather(res_low), attended),
        [pltpu.VMEM((256, D), jnp.float32)],
    )
    out_sum = z_reduce(y_sum(out_mine, out_theirs))
    own_team = (jnp.arange(4, dtype=jnp.int32) == team_pos).astype(jnp.float32)[None, :, None]
    grad_rows = jnp.concatenate(
        [
            jnp.zeros((4, D), jnp.float32),
            row_sums[:3],
            (pre_sum[0].reshape(2, 1, 512) * own_team).reshape(FF // D, D),
            row_sums[3:4],
            jnp.zeros((4, D), jnp.float32),
        ]
    )
    qkv_mine, qkv_theirs, keep, send = call(
        backward_kernel,
        "attention_backward",
        (sds((4, 144, 768)), sds((4, 144, 768), LOW), sds((256, D)), sds((256, D))),
        (at, res_team, out_weight, qkv_low, normed1, x_team, qkv_weight, seg_col, seg_ids, grad_rows),
        [
            pltpu.VMEM((TOK, 768), LOW), pltpu.VMEM((D, 768), jnp.float32),
            pltpu.VMEM((TOK, 256), LOW), pltpu.VMEM((16, D), jnp.float32),
        ],
    )
    qkv_sum = z_reduce(y_sum(qkv_mine, qkv_theirs).reshape(576, 768))
    vec_back = qkv_sum[4 * share :, :128].reshape(16, 4, 32).transpose(1, 0, 2)
    qkv_back = jnp.concatenate(
        [qkv_sum[: 4 * share].reshape(4, share, 768), jnp.pad(vec_back, ((0, 0), (0, 0), (0, 736)))], axis=1
    )
    qkv_back = team_exchange(qkv_back).astype(jnp.float32)
    up_back = team_exchange(up_sum.reshape(4, share, 1024)).astype(jnp.float32)

    summed, near = team_reduce(keep, send)
    grad_normed1 = summed + near.astype(jnp.float32)
    _, scaled1, inverse1 = normalize(x_in.astype(jnp.float32), vectors[0], vectors[1])
    grad_input = grad_residual + normalize_back(grad_normed1, scaled1, inverse1, vectors[0])
    owned = jnp.concatenate(
        [
            qkv_back[:, :share].reshape(4, share, 6, 128).transpose(1, 2, 0, 3).reshape(-1),
            out_sum.astype(jnp.float32).reshape(-1),
            up_back.reshape(4, share, 2, 512).transpose(1, 2, 0, 3).reshape(-1),
            down_sum.astype(jnp.float32).reshape(-1),
            jnp.sum(qkv_back[:, share : share + vec_rows, :32], axis=0).reshape(-1),
        ]
    )
    new_params, new_first, new_second = adam(params, first_moment, second_moment, owned, share)
    return (output, grad_input, owned, new_params, new_first, new_second)


def solution(mesh):
    shape = dict(mesh.shape)
    if shape["dp"] == 8 and shape["shard"] == 4:
        mesh = Mesh(mesh.devices.reshape(2, 2, 2, 4), ("y", "x", "c", "z"))
        axes, step = ("y", "x", "c", "z"), team_body
    else:
        axes, step = ("dp", "shard"), body
    return jax.shard_map(
        step,
        mesh=mesh,
        in_specs=(P(axes, None), P(axes, None), P(axes), P(axes), P(axes), P(), P()),
        out_specs=(P(axes, None), P(axes, None), P(axes), P(axes), P(axes), P(axes)),
        check_vma=False,
    )
```

```python
import jax
import jax.numpy as jnp
from jax import lax
from jax.experimental import pallas as pl
from jax.experimental.pallas import tpu as pltpu
from jax.sharding import Mesh
from jax.sharding import PartitionSpec as P

D = 1024
HEADS = 16
HEAD_DIM = 64
FF = 4096
STEP = 4


score_scale = 0.125
norm_eps = 1e-05
gelu_coef = 0.7978845608028654
gelu_cubic = 0.044715
learn_rate = 0.01
beta_first = 0.9
beta_second = 0.95
adam_eps = 1e-08
decay_rate = 0.1
neg_large = -1e30


def matmul(left_side, right_side):
    return jnp.dot(left_side, right_side, preferred_element_type=jnp.float32)


def matmul_tn(left_side, right_side):
    return lax.dot_general(
        left_side, right_side, (((0,), (0,)), ((), ())), preferred_element_type=jnp.float32
    )


def matmul_nt(left_side, right_side):
    return lax.dot_general(
        left_side, right_side, (((1,), (1,)), ((), ())), preferred_element_type=jnp.float32
    )


def contract(pattern, left_side, right_side):
    return jnp.einsum(pattern, left_side, right_side, preferred_element_type=jnp.float32)


def normalize(values, norm_gain, norm_shift):
    average = jnp.mean(values, axis=-1, keepdims=True)
    centered = values - average
    inverse = lax.rsqrt(jnp.mean(centered * centered, axis=-1, keepdims=True) + norm_eps)
    scaled = centered * inverse
    return (scaled * norm_gain + norm_shift, scaled, inverse)


def normalize_back(upstream, scaled, inverse, norm_gain):
    grad_scaled = upstream * norm_gain
    term_one = jnp.mean(grad_scaled, axis=-1, keepdims=True)
    term_two = jnp.mean(grad_scaled * scaled, axis=-1, keepdims=True)
    return inverse * (grad_scaled - term_one - scaled * term_two)


def gelu_parts(pre_act):
    inner_arg = gelu_coef * (pre_act + gelu_cubic * pre_act * pre_act * pre_act)
    tanh_val = jnp.tanh(inner_arg)
    act_value = 0.5 * pre_act * (1.0 + tanh_val)
    act_slope = 0.5 * (1.0 + tanh_val) + 0.5 * pre_act * (1.0 - tanh_val * tanh_val) * gelu_coef * (
        1.0 + 3.0 * gelu_cubic * pre_act * pre_act
    )
    return (act_value, act_slope)


def segments(seq_lengths, seq_device, device_ids, row_count):
    owned = seq_device[None, :] == device_ids[:, None]
    own_lengths = jnp.where(owned, seq_lengths[None, :], 0)
    ends = jnp.cumsum(own_lengths, axis=1)
    position = jnp.arange(row_count, dtype=jnp.int32)
    passed = owned[:, None, :] & (ends[:, None, :] <= position[None, :, None])
    seg_ids = jnp.sum(passed.astype(jnp.int32), axis=2)
    live_mask = position[None, :] < ends[:, -1:]
    return (seg_ids, live_mask)


def layer(x_in, cotangent, seg_ids, live_mask, weights):
    qkv_weight, out_weight, up_weight, down_weight, vectors = weights
    vectors = vectors.astype(jnp.float32)
    first_gain = vectors[0]
    first_shift = vectors[1]
    query_bias = vectors[2]
    value_bias = vectors[3]
    out_bias = vectors[4]
    second_gain = vectors[5]
    second_shift = vectors[6]
    up_bias = vectors[7 : 7 + FF // D].reshape(FF)
    down_bias = vectors[7 + FF // D]
    batch_size = x_in.shape[0]
    row_count = x_in.shape[1]
    flat_rows = batch_size * row_count
    head_shape = (batch_size, row_count, HEADS, HEAD_DIM)
    stream = x_in.astype(jnp.float32).reshape(flat_rows, D)
    normed1, scaled1, inverse1 = normalize(stream, first_gain, first_shift)
    normed1 = normed1.astype(jnp.bfloat16)
    mixed_all = matmul(normed1, qkv_weight)
    query_low = (mixed_all[:, :D] + query_bias).astype(jnp.bfloat16).reshape(head_shape)
    key_low = mixed_all[:, D : 2 * D].astype(jnp.bfloat16).reshape(head_shape)
    value_low = (mixed_all[:, 2 * D :] + value_bias).astype(jnp.bfloat16).reshape(head_shape)
    position = jnp.arange(row_count, dtype=jnp.int32)
    allowed = (seg_ids[:, :, None] == seg_ids[:, None, :]) & (
        position[None, :, None] >= position[None, None, :]
    )
    allowed = allowed[:, None, :, :]
    scores = jnp.where(
        allowed, contract("bqhe,bkhe->bhqk", query_low, key_low) * score_scale, neg_large
    )
    row_max = jnp.max(scores, axis=-1, keepdims=True)
    exp_scores = jnp.exp(scores - row_max)
    row_total = jnp.sum(exp_scores, axis=-1, keepdims=True)
    probability = exp_scores / row_total
    log_total = row_max + jnp.log(row_total)
    attended = contract("bhqk,bkhe->bqhe", probability.astype(jnp.bfloat16), value_low)
    attended = attended.astype(jnp.bfloat16).reshape(flat_rows, D)
    residual = stream + matmul(attended, out_weight) + out_bias
    normed2, scaled2, inverse2 = normalize(residual, second_gain, second_shift)
    normed2 = normed2.astype(jnp.bfloat16)
    pre_act = matmul(normed2, up_weight) + up_bias
    act_value, act_slope = gelu_parts(pre_act)
    hidden = act_value.astype(jnp.bfloat16)
    output = residual + matmul(hidden, down_weight) + down_bias
    upstream = cotangent.reshape(flat_rows, D) * live_mask.reshape(flat_rows, 1).astype(jnp.float32)
    up_low = upstream.astype(jnp.bfloat16)
    grad_down = matmul_tn(hidden, up_low)
    grad_pre = matmul_nt(up_low, down_weight) * act_slope
    pre_low = grad_pre.astype(jnp.bfloat16)
    grad_up = matmul_tn(normed2, pre_low)
    grad_normed2 = matmul_nt(pre_low, up_weight)
    grad_residual = upstream + normalize_back(grad_normed2, scaled2, inverse2, second_gain)
    res_low = grad_residual.astype(jnp.bfloat16)
    grad_out = matmul_tn(attended, res_low)
    grad_attended = matmul_nt(res_low, out_weight).astype(jnp.bfloat16).reshape(head_shape)
    scores = jnp.where(
        allowed, contract("bqhe,bkhe->bhqk", query_low, key_low) * score_scale, neg_large
    )
    probability = jnp.where(allowed, jnp.exp(scores - log_total), 0.0)
    grad_prob = contract("bqhe,bkhe->bhqk", grad_attended, value_low)
    grad_values = contract("bhqk,bqhe->bkhe", probability.astype(jnp.bfloat16), grad_attended)
    row_dot = jnp.sum(probability * grad_prob, axis=-1, keepdims=True)
    score_low = (probability * (grad_prob - row_dot)).astype(jnp.bfloat16)
    grad_queries = contract("bhqk,bkhe->bqhe", score_low, key_low) * score_scale
    grad_keys = contract("bhqk,bqhe->bkhe", score_low, query_low) * score_scale
    grad_queries = grad_queries.reshape(flat_rows, D)
    grad_keys = grad_keys.reshape(flat_rows, D)
    grad_values = grad_values.reshape(flat_rows, D)
    mixed_low = jnp.concatenate([grad_queries, grad_keys, grad_values], axis=1).astype(jnp.bfloat16)
    grad_qkv = matmul_tn(normed1, mixed_low)
    grad_normed1 = matmul_nt(mixed_low, qkv_weight)
    grad_input = grad_residual + normalize_back(grad_normed1, scaled1, inverse1, first_gain)
    head_rows = jnp.stack(
        [
            jnp.sum(grad_normed1 * scaled1, axis=0),
            jnp.sum(grad_normed1, axis=0),
            jnp.sum(grad_queries, axis=0),
            jnp.sum(grad_values, axis=0),
            jnp.sum(grad_residual, axis=0),
            jnp.sum(grad_normed2 * scaled2, axis=0),
            jnp.sum(grad_normed2, axis=0),
        ]
    )
    grad_vectors = jnp.concatenate(
        [
            head_rows,
            jnp.sum(grad_pre, axis=0).reshape(FF // D, D),
            jnp.sum(upstream, axis=0)[None, :],
        ],
        axis=0,
    )
    grads = (grad_qkv, grad_out, grad_up, grad_down, grad_vectors)
    return (
        output.reshape(batch_size, row_count, D),
        grad_input.reshape(batch_size, row_count, D),
        grads,
    )


def local_pieces(flat_slice, share):
    vec_rows = 8 + FF // D
    widths = [share * 3 * D, share * D, share * FF, share * FF, vec_rows * share]
    pieces = []
    offset = 0
    for extent in widths:
        pieces.append(lax.slice_in_dim(flat_slice, offset, offset + extent))
        offset = offset + extent
    return (
        pieces[0].reshape(share, 3 * D),
        pieces[1].reshape(share, D),
        pieces[2].reshape(share, FF),
        pieces[3].reshape(share * FF // D, D),
        pieces[4].reshape(vec_rows, share),
    )


def adam(params, first_moment, second_moment, owned, decay):
    new_first = beta_first * first_moment + (1.0 - beta_first) * owned
    new_second = beta_second * second_moment + (1.0 - beta_second) * owned * owned
    fix_first = 1.0 - beta_first**STEP
    fix_second = 1.0 - beta_second**STEP
    ratio = new_first / fix_first / (jnp.sqrt(new_second / fix_second) + adam_eps)
    new_params = params - learn_rate * (ratio + decay * params)
    return (new_params, new_first, new_second)


def body(x_in, cotangent, params, first_moment, second_moment, seq_lengths, seq_device):
    devices = lax.axis_size("dp") * lax.axis_size("shard")
    share = D // devices
    params_low = params.astype(jnp.bfloat16)
    qkv_part, out_part, up_part, down_part, vec_part = local_pieces(params_low, share)
    weights = (
        lax.all_gather(qkv_part, ("dp", "shard"), axis=0, tiled=True),
        lax.all_gather(out_part, ("dp", "shard"), axis=0, tiled=True),
        lax.all_gather(up_part, ("dp", "shard"), axis=0, tiled=True),
        lax.all_gather(down_part, ("dp", "shard"), axis=0, tiled=True),
        lax.all_gather(vec_part, ("dp", "shard"), axis=1, tiled=True),
    )
    device = lax.axis_index(("dp", "shard"))
    device_ids = jnp.reshape(device, (1,))
    seg_ids, live_mask = segments(seq_lengths, seq_device, device_ids, x_in.shape[0])
    output, grad_input, grads = layer(
        x_in[None], cotangent[None], seg_ids, live_mask, tuple(weights)
    )
    owned_parts = (
        lax.psum_scatter(grads[0], ("dp", "shard"), scatter_dimension=0, tiled=True),
        lax.psum_scatter(grads[1], ("dp", "shard"), scatter_dimension=0, tiled=True),
        lax.psum_scatter(grads[2], ("dp", "shard"), scatter_dimension=0, tiled=True),
        lax.psum_scatter(grads[3], ("dp", "shard"), scatter_dimension=0, tiled=True),
        lax.psum_scatter(grads[4], ("dp", "shard"), scatter_dimension=1, tiled=True),
    )
    owned = jnp.concatenate([piece.reshape(-1) for piece in owned_parts])
    local_index = jnp.arange(owned.shape[0], dtype=jnp.int32)
    decay = decay_rate * (local_index < share * (4 * D + 2 * FF)).astype(jnp.float32)
    new_params, new_first, new_second = adam(params, first_moment, second_moment, owned, decay)
    return (output[0], grad_input[0], owned, new_params, new_first, new_second)


SWAP = ((0, 1), (1, 0))
TEAM = ("x", "c")
LOW = jnp.bfloat16
TOK = 512
ROW = 128


def swap(values, axis):
    return lax.ppermute(values, axis, SWAP)


def z_gather(shard):
    return lax.all_gather(shard, "z", axis=0, tiled=True)


def z_reduce(values):
    return lax.psum_scatter(values, "z", scatter_dimension=0, tiled=True)


def team_exchange(values):
    return lax.all_to_all(values, TEAM, 0, 0, tiled=True)


def team_gather(own, dep=None):
    near = swap(own, "x")
    onward = near if dep is None else after(near, dep)
    return (own, near, swap(own, "c"), swap(onward, "c"))


def team_reduce(keep, send):
    recv = swap(send, "c")
    away = (keep[ROW:] + recv[ROW:]).astype(LOW)
    near = swap(away, "x")
    return (keep, recv, near)


def team_total(keep, recv, near):
    return keep[:ROW] + recv[:ROW] + near.astype(jnp.float32)


def sds(shape, dtype=jnp.float32):
    return jax.ShapeDtypeStruct(shape, dtype)


def after(value, dep):
    return lax.optimization_barrier((value, dep))[0]


def call(kernel, outs, at, operands, scratch=()):
    n_in, n_out = len(operands), len(outs)

    def staged(at_ref, *refs):
        hbm_in, hbm_out = refs[:n_in], refs[n_in : n_in + n_out]
        ins = refs[n_in + n_out : 2 * n_in + n_out]
        results = refs[2 * n_in + n_out : 2 * (n_in + n_out)]
        in_sems, out_sems = refs[-2:]
        tmp = refs[2 * (n_in + n_out) : -2]
        loads = [pltpu.make_async_copy(hbm_in[i], ins[i], in_sems.at[i]) for i in range(n_in)]
        stores = [pltpu.make_async_copy(results[i], hbm_out[i], out_sems.at[i]) for i in range(n_out)]
        waited, sent = set(), set()
        for load in loads:
            load.start()

        def ready(*which):
            for i in which or range(n_in):
                if i not in waited:
                    waited.add(i)
                    loads[i].wait()

        def flush(*which):
            for i in which or range(n_out):
                if i not in sent:
                    sent.add(i)
                    stores[i].start()

        kernel(at_ref, ins, results, tmp, ready, flush)
        ready()
        flush()
        for store in stores:
            store.wait()

    hbm = pl.BlockSpec(memory_space=pl.ANY)
    return pl.pallas_call(
        staged,
        out_shape=outs,
        in_specs=[pl.BlockSpec(memory_space=pltpu.SMEM)] + [hbm] * n_in,
        out_specs=(hbm,) * n_out,
        scratch_shapes=[pltpu.VMEM(v.shape, v.dtype) for v in operands]
        + [pltpu.VMEM(v.shape, v.dtype) for v in outs]
        + list(scratch)
        + [pltpu.SemaphoreType.DMA((n_in,)), pltpu.SemaphoreType.DMA((n_out,))],
        compiler_params=pltpu.CompilerParams(vmem_limit_bytes=60 << 20),
    )(at, *operands)


def head_lanes():
    return lax.broadcasted_iota(jnp.int32, (ROW, 128), 1) < HEAD_DIM


def lane_group(rows):
    return lax.broadcasted_iota(jnp.int32, (rows, 128), 1) // 32


def allowed_block(seg_ref, block):
    query_at = lax.broadcasted_iota(jnp.int32, (ROW, ROW), 0)
    key_at = lax.broadcasted_iota(jnp.int32, (ROW, ROW), 1)
    seg_row = seg_ref[block : block + 1, :].astype(jnp.float32)
    seg_col = jnp.sum(jnp.where(query_at == key_at, seg_row, 0.0), axis=1, keepdims=True)
    return (seg_col == seg_row) & (query_at >= key_at)


def scores_of(query_low, key_low, allowed):
    return jnp.where(allowed, matmul_nt(query_low, key_low) * score_scale, neg_large)


def forward_kernel(at, ins, outs, tmp, ready, flush):
    x_ref, own_ref, far_ref, seg_ref = ins
    vec_ref, weight_ref, out_ref, normed_ref, qkv_ref, att_ref, keep_ref, send_ref = outs
    y_pos, team = at[0], at[1]
    group = lane_group(16)
    for index, ref, side in ((1, own_ref, y_pos), (2, far_ref, 1 - y_pos)):
        ready(index)
        base = side * 512
        for z in range(4):
            for t in range(4):
                start = pl.multiple_of(base + t * 128 + z * 32, 32)
                weight_ref[pl.ds(start, 32), :] = ref[z, t * 32 : (t + 1) * 32, :]
            top = pl.multiple_of(side * 128 + z * 32, 32)
            out_ref[pl.ds(top, 32), 0:768] = ref[z, 128:160, :]
            out_ref[pl.ds(top, 16), 768:1024] = ref[z, 160:176, 0:256]
            out_ref[pl.ds(pl.multiple_of(top + 16, 16), 16), 768:1024] = ref[z, 160:176, 256:512]
        for t in range(4):
            tile = jnp.zeros((16, 128), jnp.float32)
            for z in range(4):
                piece = ref[z, 160:176, 512:640].astype(jnp.float32)
                shift = (z - t) * 32 % 128
                piece = pltpu.roll(piece, shift, 1) if shift else piece
                tile = jnp.where(group == z, piece, tile)
            vec_ref[:, pl.ds(pl.multiple_of(base + t * 128, 128), 128)] = tile
    flush(0, 1, 2)
    ready(0, 3)
    gain, shift_row = vec_ref[0:1, :], vec_ref[1:2, :]
    for block in range(4):
        rows = slice(block * ROW, (block + 1) * ROW)
        value, _, _ = normalize(x_ref[rows, :].astype(jnp.float32), gain, shift_row)
        normed_ref[rows, :] = value.astype(LOW)
    for block in range(4):
        rows = slice(block * ROW, (block + 1) * ROW)
        mixed = matmul(normed_ref[rows, :], weight_ref[...])
        for pair in range(2):
            lanes = pl.ds(pl.multiple_of(pair * 512 + team * 128, 128), 128)
            for which in range(3):
                cols = slice(which * 256 + pair * 128, which * 256 + (pair + 1) * 128)
                piece = mixed[:, cols]
                if which == 0:
                    piece = piece + vec_ref[2:3, lanes]
                if which == 2:
                    piece = piece + vec_ref[3:4, lanes]
                qkv_ref[rows, cols] = piece.astype(LOW)
    flush(3, 4)
    first = head_lanes()
    for block in range(4):
        rows = slice(block * ROW, (block + 1) * ROW)
        allowed = allowed_block(seg_ref, block)
        for pair in range(2):
            query, key, value = (
                qkv_ref[rows, w * 256 + pair * 128 : w * 256 + (pair + 1) * 128] for w in range(3)
            )
            heads = []
            for mask in (first, ~first):
                scores = scores_of(jnp.where(mask, query, jnp.zeros_like(query)), key, allowed)
                row_max = jnp.max(scores, axis=-1, keepdims=True)
                exp_scores = jnp.exp(scores - row_max)
                row_total = jnp.sum(exp_scores, axis=-1, keepdims=True)
                heads.append(matmul((exp_scores / row_total).astype(LOW), value))
            att_ref[rows, pair * 128 : (pair + 1) * 128] = jnp.where(first, heads[0], heads[1]).astype(LOW)
    send_ref[...] = matmul(att_ref[256:512, :], out_ref[...])
    flush(5, 7)
    keep_ref[...] = matmul(att_ref[0:256, :], out_ref[...])


def split_kernel(at, ins, outs, tmp, ready, flush):
    left_ref, own_ref, far_ref = ins
    keep_ref, send_ref = outs
    depth = own_ref.shape[0]
    near = pl.ds(pl.multiple_of(at[0] * depth, depth), depth)
    away = pl.ds(pl.multiple_of((1 - at[0]) * depth, depth), depth)
    ready()
    for which, ref, base in ((1, send_ref, 256), (0, keep_ref, 0)):
        rows = slice(base, base + 256)
        ref[...] = matmul(left_ref[rows, near], own_ref[...]) + matmul(left_ref[rows, away], far_ref[...])
        flush(which)


def residual_kernel(at, ins, outs, tmp, ready, flush):
    x_ref, keep_ref, recv_ref, near_ref, vec_ref = ins
    res_ref, low_ref = outs
    ready()
    total = team_total(keep_ref, recv_ref, near_ref[...])
    residual = x_ref[...].astype(jnp.float32) + total + vec_ref[4:5, :]
    res_ref[...] = residual
    value, _, _ = normalize(residual, vec_ref[5:6, :], vec_ref[6:7, :])
    low_ref[...] = value.astype(LOW)


def up_kernel(at, ins, outs, tmp, ready, flush):
    n0, n1, n2, n3, own_ref, far_ref, vec_ref, uplow_ref = ins
    team = at[1]
    team_ref, weight_ref, hidden_ref, slope_ref, mine_ref, theirs_ref = outs
    grad_ref, = tmp
    ready(4, 5, 6, 0, 1, 2, 3)
    y_pos = at[0]
    for block, ref in enumerate((n0, n1, n2, n3)):
        team_ref[block * ROW : (block + 1) * ROW, :] = ref[...]
    for ref, side in ((own_ref, y_pos), (far_ref, 1 - y_pos)):
        for z in range(4):
            for t in range(4):
                start = pl.multiple_of(side * 512 + t * 128 + z * 32, 32)
                weight_ref[pl.ds(start, 32), :] = ref[z, t * 32 : (t + 1) * 32, :]
    flush(0, 1)
    bias_lanes = pl.ds(pl.multiple_of((team % 2) * 512, 512), 512)
    bias = jnp.concatenate([vec_ref[pl.ds(7 + 2 * side + team // 2, 1), bias_lanes] for side in range(2)], axis=1)
    for block in range(4):
        rows = slice(block * ROW, (block + 1) * ROW)
        pre_act = matmul(team_ref[rows, :], weight_ref[...]) + bias
        act_value, act_slope = gelu_parts(pre_act)
        hidden_ref[rows, :] = act_value.astype(LOW)
        slope_ref[rows, :] = act_slope
    flush(2, 3)
    ready(7)
    grad_ref[...] = matmul_tn(hidden_ref[...], uplow_ref[...])
    mine_ref[...] = grad_ref[pl.ds(pl.multiple_of(y_pos * 512, 512), 512), :]
    theirs_ref[...] = grad_ref[pl.ds(pl.multiple_of((1 - y_pos) * 512, 512), 512), :].astype(LOW)


def down_kernel(at, ins, outs, tmp, ready, flush):
    uplow_ref, own_ref, far_ref, slope_ref, weight_ref = ins
    pre_ref, sum_ref, keep_ref, send_ref = outs
    ready(0, 1, 2, 3)
    y_pos = at[0]
    sum_ref[...] = jnp.zeros_like(sum_ref)
    for ref, side in ((own_ref, y_pos), (far_ref, 1 - y_pos)):
        cols = pl.ds(pl.multiple_of(side * 512, 512), 512)
        for block in range(4):
            rows = slice(block * ROW, (block + 1) * ROW)
            grad_pre = matmul_nt(uplow_ref[rows, :], ref[...]) * slope_ref[rows, cols]
            pre_ref[rows, cols] = grad_pre.astype(LOW)
            sum_ref[0:1, cols] += jnp.sum(grad_pre, axis=0, keepdims=True)
    flush(0, 1)
    ready(4)
    send_ref[...] = matmul_nt(pre_ref[256:512, :], weight_ref[...])
    flush(3)
    keep_ref[...] = matmul_nt(pre_ref[0:256, :], weight_ref[...])


def spread(at, grad_ref, mine_ref, theirs_ref):
    y_pos = at[0]
    for z in range(4):
        for t in range(4):
            near = pl.multiple_of(y_pos * 512 + t * 128 + z * 32, 32)
            away = pl.multiple_of((1 - y_pos) * 512 + t * 128 + z * 32, 32)
            mine_ref[z, t * 32 : (t + 1) * 32, :] = grad_ref[pl.ds(near, 32), :]
            theirs_ref[z, t * 32 : (t + 1) * 32, :] = grad_ref[pl.ds(away, 32), :].astype(LOW)


def up_grad_kernel(at, ins, outs, tmp, ready, flush):
    team_ref, pre_ref = ins
    mine_ref, theirs_ref = outs
    grad_ref, = tmp
    ready()
    grad_ref[...] = matmul_tn(team_ref[...], pre_ref[...])
    spread(at, grad_ref, mine_ref, theirs_ref)


def residual_back_kernel(at, ins, outs, tmp, ready, flush):
    res_ref, keep_ref, recv_ref, near_ref, up_ref, vec_ref = ins
    grad_ref, low_ref, rows_ref = outs
    ready()
    _, scaled, inverse = normalize(res_ref[...], vec_ref[5:6, :], vec_ref[6:7, :])
    grad_normed = team_total(keep_ref, recv_ref, near_ref[...])
    upstream = up_ref[...]
    grad = upstream + normalize_back(grad_normed, scaled, inverse, vec_ref[5:6, :])
    grad_ref[...] = grad
    low_ref[...] = grad.astype(LOW)
    total = lambda value: jnp.sum(value, axis=0, keepdims=True)
    rows_ref[...] = jnp.zeros_like(rows_ref)
    rows_ref[0:1, :] = total(grad)
    rows_ref[1:2, :] = total(grad_normed * scaled)
    rows_ref[2:3, :] = total(grad_normed)
    rows_ref[3:4, :] = total(upstream)


def out_grad_kernel(at, ins, outs, tmp, ready, flush):
    att_ref = ins[4]
    mine_ref, theirs_ref = outs
    ready(4)
    for ref, side in ((theirs_ref, 1 - at[0]), (mine_ref, at[0])):
        cols = pl.ds(pl.multiple_of(side * 128, 128), 128)
        total = jnp.zeros((128, D), jnp.float32)
        for block in range(4):
            ready(block)
            total = total + matmul_tn(att_ref[block * ROW : (block + 1) * ROW, cols], ins[block][...])
        ref[...] = total.astype(ref.dtype)


def backward_kernel(at, ins, outs, tmp, ready, flush):
    out_ref, qkv_ref, seg_ref, normed_ref = ins[4:]
    mine_ref, theirs_ref, mixed_ref, bias_ref = outs
    grad_ref, att_ref = tmp
    ready(4)
    for block in range(4):
        ready(block)
        att_ref[block * ROW : (block + 1) * ROW, :] = matmul_nt(ins[block][...], out_ref[...]).astype(LOW)
    ready(5, 6)
    bias_ref[...] = jnp.zeros_like(bias_ref)
    first = head_lanes()
    for pair in range(2):
        query_sum = jnp.zeros((1, 128), jnp.float32)
        value_sum = jnp.zeros((1, 128), jnp.float32)
        for block in range(4):
            rows = slice(block * ROW, (block + 1) * ROW)
            allowed = allowed_block(seg_ref, block)
            query, key, value = (
                qkv_ref[rows, w * 256 + pair * 128 : w * 256 + (pair + 1) * 128] for w in range(3)
            )
            grad_att = att_ref[rows, pair * 128 : (pair + 1) * 128]
            parts = []
            for mask in (first, ~first):
                scores = scores_of(jnp.where(mask, query, jnp.zeros_like(query)), key, allowed)
                row_max = jnp.max(scores, axis=-1, keepdims=True)
                log_total = row_max + jnp.log(jnp.sum(jnp.exp(scores - row_max), axis=-1, keepdims=True))
                probability = jnp.where(allowed, jnp.exp(scores - log_total), 0.0)
                grad_prob = matmul_nt(jnp.where(mask, grad_att, jnp.zeros_like(grad_att)), value)
                grad_value = matmul_tn(probability.astype(LOW), grad_att)
                row_dot = jnp.sum(probability * grad_prob, axis=-1, keepdims=True)
                score_low = (probability * (grad_prob - row_dot)).astype(LOW)
                parts.append(
                    (matmul(score_low, key) * score_scale, matmul_tn(score_low, query) * score_scale, grad_value)
                )
            for which in range(3):
                merged = jnp.where(first, parts[0][which], parts[1][which])
                mixed_ref[rows, which * 256 + pair * 128 : which * 256 + (pair + 1) * 128] = merged.astype(LOW)
                if which == 0:
                    query_sum = query_sum + jnp.sum(merged, axis=0, keepdims=True)
                if which == 2:
                    value_sum = value_sum + jnp.sum(merged, axis=0, keepdims=True)
        bias_ref[0:1, pair * 128 : (pair + 1) * 128] = query_sum
        bias_ref[1:2, pair * 128 : (pair + 1) * 128] = value_sum
    flush(2, 3)
    ready()
    grad_ref[...] = matmul_tn(normed_ref[...], mixed_ref[...])
    spread(at, grad_ref, mine_ref, theirs_ref)


def vector_kernel(at, ins, outs, tmp, ready, flush):
    mixed_ref, weight_ref, x_ref, rows_ref, pre_ref, bias_ref = ins
    mine_ref, theirs_ref, keep_ref, send_ref = outs
    vec_ref, = tmp
    y_pos, team = at[0], at[1]
    ready()
    vec_ref[...] = jnp.zeros_like(vec_ref)
    vec_ref[4:7, :] = rows_ref[0:3, :]
    vec_ref[11:12, :] = rows_ref[3:4, :]
    for side in range(2):
        at_row = pl.ds(7 + 2 * side + team // 2, 1)
        vec_ref[at_row, pl.ds(pl.multiple_of((team % 2) * 512, 512), 512)] = pre_ref[0:1, side * 512 : (side + 1) * 512]
        lanes = pl.ds(pl.multiple_of(side * 512 + team * 128, 128), 128)
        vec_ref[2:4, lanes] = bias_ref[0:2, side * 128 : (side + 1) * 128]
    send_ref[...] = matmul_nt(mixed_ref[256:512, :], weight_ref[...])
    flush(3)
    keep_ref[...] = matmul_nt(mixed_ref[0:256, :], weight_ref[...])
    flush(2)
    gain_sum = jnp.zeros((1, D), jnp.float32)
    shift_sum = jnp.zeros((1, D), jnp.float32)
    for block in range(4):
        rows = slice(block * ROW, (block + 1) * ROW)
        _, scaled, _ = normalize(x_ref[rows, :].astype(jnp.float32), 1.0, 0.0)
        source, at_row = (keep_ref, block) if block < 2 else (send_ref, block - 2)
        partial = source[at_row * ROW : (at_row + 1) * ROW, :]
        gain_sum = gain_sum + jnp.sum(partial * scaled, axis=0, keepdims=True)
        shift_sum = shift_sum + jnp.sum(partial, axis=0, keepdims=True)
    vec_ref[0:1, :] = gain_sum
    vec_ref[1:2, :] = shift_sum
    group = lane_group(16)
    for ref, side, kind in ((mine_ref, y_pos, jnp.float32), (theirs_ref, 1 - y_pos, LOW)):
        for z in range(4):
            tile = jnp.zeros((16, 128), jnp.float32)
            for t in range(4):
                piece = vec_ref[:, pl.ds(pl.multiple_of(side * 512 + t * 128, 128), 128)]
                shift = (t - z) * 32 % 128
                piece = pltpu.roll(piece, shift, 1) if shift else piece
                tile = jnp.where(group == t, piece, tile)
            ref[z] = tile.astype(kind)


def fold_kernel(at, ins, outs, tmp, ready, flush):
    mine_ref, recv_ref, vec_mine, vec_recv = ins
    ready()
    for hop in (1, 2, 3, 0):
        dest = lax.rem(at[2] + hop, 4)
        ref = outs[hop]
        ref[0:128, :] = (mine_ref[dest] + recv_ref[dest].astype(jnp.float32)).astype(ref.dtype)
        ref[128:144, 0:128] = (vec_mine[dest] + vec_recv[dest].astype(jnp.float32)).astype(ref.dtype)
        ref[128:144, 128:768] = jnp.zeros((16, 640), ref.dtype)
        flush(hop)


def step_rows(params_ref, first_ref, second_ref, grad_ref, new_refs, start, count, chunk, decay):
    def visit(index, carry):
        rows = pl.ds(pl.multiple_of(start + index * chunk, 8), chunk)
        outs = adam(params_ref[rows, :], first_ref[rows, :], second_ref[rows, :], grad_ref[rows, :], decay)
        for ref, value in zip(new_refs, outs):
            ref[rows, :] = value
        return carry

    lax.fori_loop(0, count // chunk, visit, 0)


def run_copies(pairs, sems, base):
    copies = [pltpu.make_async_copy(src, dst, sems.at[base + i]) for i, (src, dst) in enumerate(pairs)]
    for copy in copies:
        copy.start()
    for copy in copies:
        copy.wait()


def early_kernel(at, p_hbm, m_hbm, v_hbm, up_hbm, down_hbm, *refs):
    hbm_outs = refs[:4]
    p_ref, m_ref, v_ref, up_ref, down_ref, g_ref, np_ref, nm_ref, nv_ref, sems = refs[4:]
    part = lambda ref: ref.at[pl.ds(1024, 2048), :]
    pairs = [(up_hbm, up_ref), (down_hbm, down_ref)]
    pairs.extend((part(hbm), ref) for hbm, ref in ((p_hbm, p_ref), (m_hbm, m_ref), (v_hbm, v_ref)))
    run_copies(pairs, sems, 0)
    for j in range(8):
        cols = slice(j * 128, (j + 1) * 128)
        g_ref[pl.ds(1024 + j, 128, stride=8), :] = down_ref[:, cols].astype(jnp.float32)
        for t in range(4):
            flat = (j // 4) * 16 + t * 4 + j % 4
            g_ref[pl.ds(flat, 32, stride=32), :] = up_ref[t, :, cols].astype(jnp.float32)
    step_rows(p_ref, m_ref, v_ref, g_ref, (np_ref, nm_ref, nv_ref), 0, 2048, 128, decay_rate)
    run_copies([(src, part(dst)) for src, dst in zip((g_ref, np_ref, nm_ref, nv_ref), hbm_outs)], sems, 5)


def late_kernel(at, p_hbm, m_hbm, v_hbm, qkv_hbm, out_hbm, *refs):
    hbm_outs = refs[4:8]
    p_ref, m_ref, v_ref, qkv_ref, out_ref, g_ref, np_ref, nm_ref, nv_ref, sems = refs[8:]
    spans = lambda ref, hbm: (
        (hbm.at[pl.ds(0, 1024), :], ref.at[pl.ds(0, 1024), :]),
        (hbm.at[pl.ds(3072, 3), :], ref.at[pl.ds(1024, 3), :]),
    )
    pairs = [(qkv_hbm, qkv_ref), (out_hbm, out_ref)]
    for hbm, ref in ((p_hbm, p_ref), (m_hbm, m_ref), (v_hbm, v_ref)):
        pairs.extend(spans(ref, hbm))
    run_copies(pairs, sems, 0)
    for g in range(6):
        for t in range(4):
            g_ref[pl.ds(g * 4 + t, 32, stride=24), :] = qkv_ref[t, 0:32, g * 128 : (g + 1) * 128].astype(jnp.float32)
    for j in range(8):
        g_ref[pl.ds(768 + j, 32, stride=8), :] = out_ref[:, j * 128 : (j + 1) * 128].astype(jnp.float32)
    total = jnp.zeros((16, 128), jnp.float32)
    for t in range(4):
        total = total + qkv_ref[t, 32:48, 0:128].astype(jnp.float32)
    group = lane_group(1)
    turned = [pltpu.roll(total, q * 32, 1) if q else total for q in range(4)]
    for r in range(3):
        row = jnp.zeros((1, 128), jnp.float32)
        for q in range(4):
            row = jnp.where(group == q, turned[q][4 * r + q : 4 * r + q + 1, :], row)
        g_ref[1024 + r : 1025 + r, :] = row
    new_refs = (np_ref, nm_ref, nv_ref)
    step_rows(p_ref, m_ref, v_ref, g_ref, new_refs, 0, 1024, 128, decay_rate)
    tail = slice(1024, 1027)
    outs = adam(p_ref[tail, :], m_ref[tail, :], v_ref[tail, :], g_ref[tail, :], 0.0)
    for ref, value in zip(new_refs, outs):
        ref[tail, :] = value
    pairs = []
    for hbm, ref in zip(hbm_outs, (g_ref,) + new_refs):
        pairs.extend((src, dst) for dst, src in spans(ref, hbm))
    run_copies(pairs, sems, 8)


def adam_call(kernel, at, arrays, previous, rows, extra_sems):
    hbm = pl.BlockSpec(memory_space=pltpu.HBM)
    operands = tuple(arrays) + tuple(previous)
    grads = [pltpu.VMEM(v.shape, v.dtype) for v in arrays[3:]]
    block = pltpu.VMEM((rows, 128), jnp.float32)
    return pl.pallas_call(
        kernel,
        out_shape=tuple(sds(arrays[0].shape) for _ in range(4)),
        in_specs=[pl.BlockSpec(memory_space=pltpu.SMEM)] + [hbm] * len(operands),
        out_specs=(hbm,) * 4,
        scratch_shapes=[block] * 3 + grads + [block] * 4 + [pltpu.SemaphoreType.DMA((extra_sems,))],
        input_output_aliases={1 + len(arrays) + i: i for i in range(len(previous))},
        compiler_params=pltpu.CompilerParams(vmem_limit_bytes=60 << 20),
    )(at, *operands)


def join_kernel(at, ins, outs, tmp, ready, flush):
    own_ref, r1, r2, r3 = ins
    pay_ref, = outs
    ready()
    total = own_ref[...]
    for ref in (r1, r2, r3):
        total = total + ref[...].astype(jnp.float32)
    for t in range(4):
        pay_ref[t, 0:32, :] = total[t * 32 : (t + 1) * 32, :].astype(LOW)
        tile = total[128:144, 0:128]
        pay_ref[t, 32:48, 0:128] = (pltpu.roll(tile, 128 - t * 32, 1) if t else tile).astype(LOW)
        pay_ref[t, 32:48, 128:768] = jnp.zeros((16, 640), LOW)


def team_body(*arrays):
    return team_step(*arrays)


def team_step(x_in, cotangent, params, first_moment, second_moment, seq_lengths, seq_device):
    rows = x_in.shape[0]
    share = D // 32
    y_pos = lax.axis_index("y")
    x_pos = lax.axis_index("x")
    c_pos = lax.axis_index("c")
    z_pos = lax.axis_index("z")
    team_pos = x_pos * 2 + c_pos
    at = jnp.stack([y_pos, team_pos, z_pos]).astype(jnp.int32)

    qkv_part, out_part, up_part, down_part, vec_part = local_pieces(params.astype(LOW), share)
    qkv_send = qkv_part.reshape(share, 6, 4, 128).transpose(2, 0, 1, 3).reshape(4, share, 768)
    vec_row = jnp.broadcast_to(jnp.pad(vec_part, ((0, 4), (0, 736)))[None], (4, 16, 768))
    qkv_team = team_exchange(jnp.concatenate([qkv_send, vec_row], axis=1))
    vec_team = qkv_team[:, share:, :32].transpose(1, 0, 2).reshape(16, 128)
    rest = jnp.concatenate(
        [out_part[:16, 768:], out_part[16:, 768:], vec_team, jnp.zeros((16, 128), LOW)], axis=1
    )
    qkv_shard = jnp.concatenate([qkv_team[:, :share].reshape(4 * share, 768), out_part[:, :768], rest])
    qkv_own = z_gather(qkv_shard).reshape(4, 176, 768)
    qkv_far = swap(qkv_own, "y")
    up_send = up_part.reshape(share, 2, 4, 512).transpose(2, 0, 1, 3).reshape(4, share, 1024)
    up_team = team_exchange(after(up_send, qkv_shard))
    up_own = z_gather(up_team.reshape(4 * share, 1024)).reshape(4, 4 * share, 1024)
    up_far = swap(up_own, "y")
    down_own = z_gather(after(down_part, up_team))

    steps = jnp.arange(2, dtype=jnp.int32)
    team_devices = (
        ((y_pos * 2 + (x_pos ^ steps[None, :])) * 2 + (c_pos ^ steps[:, None])) * 4 + z_pos
    ).reshape(4)
    seg_ids, live_mask = segments(seq_lengths, seq_device, team_devices.astype(jnp.int32), rows)

    upstream = cotangent * live_mask[0][:, None].astype(jnp.float32)
    token_pack = after(jnp.stack([x_in, upstream.astype(LOW)]), up_team)
    tokens = jnp.stack(team_gather(token_pack))
    x_team = tokens[:, 0].reshape(TOK, D)
    up_low = tokens[:, 1].reshape(TOK, D)

    vectors, qkv_weight, out_weight, normed1, qkv_low, attended, keep, send = call(
        forward_kernel,
        (
            sds((16, D)), sds((D, 768), LOW), sds((256, D), LOW), sds((TOK, D), LOW),
            sds((TOK, 768), LOW), sds((TOK, 256), LOW), sds((256, D)), sds((256, D)),
        ),
        at,
        (x_team, qkv_own, qkv_far, seg_ids),
    )
    keep, recv, near = team_reduce(keep, send)
    residual, normed2 = call(
        residual_kernel, (sds((rows, D)), sds((rows, D), LOW)), at, (x_in, keep, recv, near, vectors)
    )
    norm_blocks = team_gather(normed2)
    down_far = swap(after(down_own, normed2), "y")
    normed2, up_weight, hidden, slope, down_mine, down_theirs = call(
        up_kernel,
        (
            sds((TOK, D), LOW), sds((D, 1024), LOW), sds((TOK, 1024), LOW), sds((TOK, 1024)),
            sds((512, D)), sds((512, D), LOW),
        ),
        at,
        (*norm_blocks, up_own, up_far, vectors, up_low),
        [pltpu.VMEM((1024, D), jnp.float32)],
    )
    down_recv = swap(down_theirs, "y")
    pre_low, pre_sum, keep, send = call(
        down_kernel,
        (sds((TOK, 1024), LOW), sds((8, 1024)), sds((256, D)), sds((256, D))),
        at,
        (up_low, down_own, down_far, slope, up_weight),
    )
    keep, recv, near = team_reduce(keep, send)
    y_sum = lambda mine, recv: (mine + recv.astype(jnp.float32)).astype(LOW)
    down_pay = y_sum(after(down_mine, pre_sum), down_recv)
    down_sum = z_reduce(down_pay)
    grad_residual, res_low, row_sums = call(
        residual_back_kernel,
        (sds((rows, D)), sds((rows, D), LOW), sds((8, D))),
        at,
        (residual, keep, recv, after(near, down_pay), upstream, vectors),
    )
    up_mine, up_theirs = call(
        up_grad_kernel,
        (sds((4, 4 * share, 1024)), sds((4, 4 * share, 1024), LOW)),
        at,
        (normed2, after(pre_low, res_low)),
        [pltpu.VMEM((D, 1024), jnp.float32)],
    )
    up_recv = swap(up_theirs, "y")
    res_blocks = team_gather(res_low, up_theirs)
    out_mine, out_theirs = call(out_grad_kernel, (sds((128, D)), sds((128, D), LOW)), at, (*res_blocks, attended))
    out_recv = swap(out_theirs, "y")
    qkv_mine, qkv_theirs, mixed_low, bias_sums = call(
        backward_kernel,
        (sds((4, 128, 768)), sds((4, 128, 768), LOW), sds((TOK, 768), LOW), sds((8, 256))),
        at,
        (*res_blocks, out_weight, qkv_low, seg_ids, normed1),
        [pltpu.VMEM((D, 768), jnp.float32), pltpu.VMEM((TOK, 256), LOW)],
    )
    qkv_recv = swap(qkv_theirs, "y")
    vec_mine, vec_theirs, keep, send = call(
        vector_kernel,
        (sds((4, 16, 128)), sds((4, 16, 128), LOW), sds((256, D)), sds((256, D))),
        at,
        (mixed_low, qkv_weight, x_team, row_sums, pre_sum, bias_sums),
        [pltpu.VMEM((16, D), jnp.float32)],
    )
    vec_recv = swap(vec_theirs, "y")
    up_pay = y_sum(after(up_mine, qkv_theirs), up_recv).reshape(TOK, D)
    up_sum = z_reduce(up_pay)
    out_sum = z_reduce(y_sum(after(out_mine, qkv_theirs), out_recv))
    own, *pieces = call(
        fold_kernel, (sds((144, 768)),) + (sds((144, 768), LOW),) * 3, at, (qkv_mine, qkv_recv, vec_mine, vec_recv)
    )
    up_back = team_exchange(after(up_sum, own).reshape(4, share, 1024))
    turned = [
        lax.ppermute(piece, "z", [(i, (i + hop) % 4) for i in range(4)])
        for hop, piece in zip((1, 2, 3), pieces)
    ]

    final_keep, final_send = keep, send
    keep, send = call(
        split_kernel, (sds((256, D)), sds((256, D))), at,
        (after(hidden, vec_theirs), down_own, down_far),
    )
    output = residual + team_total(*team_reduce(keep, send)) + vectors[7 + FF // D]
    grad_normed1 = team_total(*team_reduce(final_keep, final_send))
    _, scaled1, inverse1 = normalize(x_in.astype(jnp.float32), vectors[0], vectors[1])
    grad_input = grad_residual + normalize_back(grad_normed1, scaled1, inverse1, vectors[0])

    state = tuple(v.reshape(-1, 128) for v in (params, first_moment, second_moment))
    early = adam_call(early_kernel, at, (*state, up_back, down_sum), (), 2048, 9)
    (qkv_pay,) = call(join_kernel, (sds((4, 48, 768), LOW),), at, (after(own, early[0]), *turned))
    qkv_back = team_exchange(qkv_pay)
    final = adam_call(late_kernel, at, (*state, qkv_back, out_sum), early, 1032, 16)
    owned, new_params, new_first, new_second = (v.reshape(-1) for v in final)
    return (output, grad_input, owned, new_params, new_first, new_second)


def solution(mesh):
    shape = dict(mesh.shape)
    if shape["dp"] == 8 and shape["shard"] == 4:
        mesh = Mesh(mesh.devices.reshape(2, 2, 2, 4), ("y", "x", "c", "z"))
        axes, step = ("y", "x", "c", "z"), team_body
    else:
        axes, step = ("dp", "shard"), body
    mapped = jax.shard_map(
        step,
        mesh=mesh,
        in_specs=(P(axes, None), P(axes, None), P(axes), P(axes), P(axes), P(), P()),
        out_specs=(P(axes, None), P(axes, None), P(axes), P(axes), P(axes), P(axes)),
        check_vma=False,
    )
    if step is body:
        return mapped
    return mapped
```

```python
import jax
import jax.numpy as jnp
from jax import lax
from jax.experimental import pallas as pl
from jax.experimental.pallas import tpu as pltpu
from jax.sharding import Mesh
from jax.sharding import PartitionSpec as P

D = 1024
HEADS = 16
HEAD_DIM = 64
FF = 4096
STEP = 4


score_scale = 0.125
norm_eps = 1e-05
gelu_coef = 0.7978845608028654
gelu_cubic = 0.044715
learn_rate = 0.01
beta_first = 0.9
beta_second = 0.95
adam_eps = 1e-08
decay_rate = 0.1
neg_large = -1e30


def matmul(left_side, right_side):
    return jnp.dot(left_side, right_side, preferred_element_type=jnp.float32)


def matmul_tn(left_side, right_side):
    return lax.dot_general(
        left_side, right_side, (((0,), (0,)), ((), ())), preferred_element_type=jnp.float32
    )


def matmul_nt(left_side, right_side):
    return lax.dot_general(
        left_side, right_side, (((1,), (1,)), ((), ())), preferred_element_type=jnp.float32
    )


def contract(pattern, left_side, right_side):
    return jnp.einsum(pattern, left_side, right_side, preferred_element_type=jnp.float32)


def normalize(values, norm_gain, norm_shift):
    average = jnp.mean(values, axis=-1, keepdims=True)
    centered = values - average
    inverse = lax.rsqrt(jnp.mean(centered * centered, axis=-1, keepdims=True) + norm_eps)
    scaled = centered * inverse
    return (scaled * norm_gain + norm_shift, scaled, inverse)


def normalize_back(upstream, scaled, inverse, norm_gain):
    grad_scaled = upstream * norm_gain
    term_one = jnp.mean(grad_scaled, axis=-1, keepdims=True)
    term_two = jnp.mean(grad_scaled * scaled, axis=-1, keepdims=True)
    return inverse * (grad_scaled - term_one - scaled * term_two)


def gelu_parts(pre_act):
    inner_arg = gelu_coef * (pre_act + gelu_cubic * pre_act * pre_act * pre_act)
    tanh_val = jnp.tanh(inner_arg)
    act_value = 0.5 * pre_act * (1.0 + tanh_val)
    act_slope = 0.5 * (1.0 + tanh_val) + 0.5 * pre_act * (1.0 - tanh_val * tanh_val) * gelu_coef * (
        1.0 + 3.0 * gelu_cubic * pre_act * pre_act
    )
    return (act_value, act_slope)


def segments(seq_lengths, seq_device, device_ids, row_count):
    owned = seq_device[None, :] == device_ids[:, None]
    own_lengths = jnp.where(owned, seq_lengths[None, :], 0)
    ends = jnp.cumsum(own_lengths, axis=1)
    position = jnp.arange(row_count, dtype=jnp.int32)
    passed = owned[:, None, :] & (ends[:, None, :] <= position[None, :, None])
    seg_ids = jnp.sum(passed.astype(jnp.int32), axis=2)
    live_mask = position[None, :] < ends[:, -1:]
    return (seg_ids, live_mask)


def layer(x_in, cotangent, seg_ids, live_mask, weights):
    qkv_weight, out_weight, up_weight, down_weight, vectors = weights
    vectors = vectors.astype(jnp.float32)
    first_gain = vectors[0]
    first_shift = vectors[1]
    query_bias = vectors[2]
    value_bias = vectors[3]
    out_bias = vectors[4]
    second_gain = vectors[5]
    second_shift = vectors[6]
    up_bias = vectors[7 : 7 + FF // D].reshape(FF)
    down_bias = vectors[7 + FF // D]
    batch_size = x_in.shape[0]
    row_count = x_in.shape[1]
    flat_rows = batch_size * row_count
    head_shape = (batch_size, row_count, HEADS, HEAD_DIM)
    stream = x_in.astype(jnp.float32).reshape(flat_rows, D)
    normed1, scaled1, inverse1 = normalize(stream, first_gain, first_shift)
    normed1 = normed1.astype(jnp.bfloat16)
    mixed_all = matmul(normed1, qkv_weight)
    query_low = (mixed_all[:, :D] + query_bias).astype(jnp.bfloat16).reshape(head_shape)
    key_low = mixed_all[:, D : 2 * D].astype(jnp.bfloat16).reshape(head_shape)
    value_low = (mixed_all[:, 2 * D :] + value_bias).astype(jnp.bfloat16).reshape(head_shape)
    position = jnp.arange(row_count, dtype=jnp.int32)
    allowed = (seg_ids[:, :, None] == seg_ids[:, None, :]) & (
        position[None, :, None] >= position[None, None, :]
    )
    allowed = allowed[:, None, :, :]
    scores = jnp.where(
        allowed, contract("bqhe,bkhe->bhqk", query_low, key_low) * score_scale, neg_large
    )
    row_max = jnp.max(scores, axis=-1, keepdims=True)
    exp_scores = jnp.exp(scores - row_max)
    row_total = jnp.sum(exp_scores, axis=-1, keepdims=True)
    probability = exp_scores / row_total
    log_total = row_max + jnp.log(row_total)
    attended = contract("bhqk,bkhe->bqhe", probability.astype(jnp.bfloat16), value_low)
    attended = attended.astype(jnp.bfloat16).reshape(flat_rows, D)
    residual = stream + matmul(attended, out_weight) + out_bias
    normed2, scaled2, inverse2 = normalize(residual, second_gain, second_shift)
    normed2 = normed2.astype(jnp.bfloat16)
    pre_act = matmul(normed2, up_weight) + up_bias
    act_value, act_slope = gelu_parts(pre_act)
    hidden = act_value.astype(jnp.bfloat16)
    output = residual + matmul(hidden, down_weight) + down_bias
    upstream = cotangent.reshape(flat_rows, D) * live_mask.reshape(flat_rows, 1).astype(jnp.float32)
    up_low = upstream.astype(jnp.bfloat16)
    grad_down = matmul_tn(hidden, up_low)
    grad_pre = matmul_nt(up_low, down_weight) * act_slope
    pre_low = grad_pre.astype(jnp.bfloat16)
    grad_up = matmul_tn(normed2, pre_low)
    grad_normed2 = matmul_nt(pre_low, up_weight)
    grad_residual = upstream + normalize_back(grad_normed2, scaled2, inverse2, second_gain)
    res_low = grad_residual.astype(jnp.bfloat16)
    grad_out = matmul_tn(attended, res_low)
    grad_attended = matmul_nt(res_low, out_weight).astype(jnp.bfloat16).reshape(head_shape)
    scores = jnp.where(
        allowed, contract("bqhe,bkhe->bhqk", query_low, key_low) * score_scale, neg_large
    )
    probability = jnp.where(allowed, jnp.exp(scores - log_total), 0.0)
    grad_prob = contract("bqhe,bkhe->bhqk", grad_attended, value_low)
    grad_values = contract("bhqk,bqhe->bkhe", probability.astype(jnp.bfloat16), grad_attended)
    row_dot = jnp.sum(probability * grad_prob, axis=-1, keepdims=True)
    score_low = (probability * (grad_prob - row_dot)).astype(jnp.bfloat16)
    grad_queries = contract("bhqk,bkhe->bqhe", score_low, key_low) * score_scale
    grad_keys = contract("bhqk,bqhe->bkhe", score_low, query_low) * score_scale
    grad_queries = grad_queries.reshape(flat_rows, D)
    grad_keys = grad_keys.reshape(flat_rows, D)
    grad_values = grad_values.reshape(flat_rows, D)
    mixed_low = jnp.concatenate([grad_queries, grad_keys, grad_values], axis=1).astype(jnp.bfloat16)
    grad_qkv = matmul_tn(normed1, mixed_low)
    grad_normed1 = matmul_nt(mixed_low, qkv_weight)
    grad_input = grad_residual + normalize_back(grad_normed1, scaled1, inverse1, first_gain)
    head_rows = jnp.stack(
        [
            jnp.sum(grad_normed1 * scaled1, axis=0),
            jnp.sum(grad_normed1, axis=0),
            jnp.sum(grad_queries, axis=0),
            jnp.sum(grad_values, axis=0),
            jnp.sum(grad_residual, axis=0),
            jnp.sum(grad_normed2 * scaled2, axis=0),
            jnp.sum(grad_normed2, axis=0),
        ]
    )
    grad_vectors = jnp.concatenate(
        [
            head_rows,
            jnp.sum(grad_pre, axis=0).reshape(FF // D, D),
            jnp.sum(upstream, axis=0)[None, :],
        ],
        axis=0,
    )
    grads = (grad_qkv, grad_out, grad_up, grad_down, grad_vectors)
    return (
        output.reshape(batch_size, row_count, D),
        grad_input.reshape(batch_size, row_count, D),
        grads,
    )


def local_pieces(flat_slice, share):
    vec_rows = 8 + FF // D
    widths = [share * 3 * D, share * D, share * FF, share * FF, vec_rows * share]
    pieces = []
    offset = 0
    for extent in widths:
        pieces.append(lax.slice_in_dim(flat_slice, offset, offset + extent))
        offset = offset + extent
    return (
        pieces[0].reshape(share, 3 * D),
        pieces[1].reshape(share, D),
        pieces[2].reshape(share, FF),
        pieces[3].reshape(share * FF // D, D),
        pieces[4].reshape(vec_rows, share),
    )


def adam(params, first_moment, second_moment, owned, decay):
    new_first = beta_first * first_moment + (1.0 - beta_first) * owned
    new_second = beta_second * second_moment + (1.0 - beta_second) * owned * owned
    fix_first = 1.0 - beta_first**STEP
    fix_second = 1.0 - beta_second**STEP
    ratio = new_first / fix_first / (jnp.sqrt(new_second / fix_second) + adam_eps)
    new_params = params - learn_rate * (ratio + decay * params)
    return (new_params, new_first, new_second)


def body(x_in, cotangent, params, first_moment, second_moment, seq_lengths, seq_device):
    devices = lax.axis_size("dp") * lax.axis_size("shard")
    share = D // devices
    params_low = params.astype(jnp.bfloat16)
    qkv_part, out_part, up_part, down_part, vec_part = local_pieces(params_low, share)
    weights = (
        lax.all_gather(qkv_part, ("dp", "shard"), axis=0, tiled=True),
        lax.all_gather(out_part, ("dp", "shard"), axis=0, tiled=True),
        lax.all_gather(up_part, ("dp", "shard"), axis=0, tiled=True),
        lax.all_gather(down_part, ("dp", "shard"), axis=0, tiled=True),
        lax.all_gather(vec_part, ("dp", "shard"), axis=1, tiled=True),
    )
    device = lax.axis_index(("dp", "shard"))
    device_ids = jnp.reshape(device, (1,))
    seg_ids, live_mask = segments(seq_lengths, seq_device, device_ids, x_in.shape[0])
    output, grad_input, grads = layer(
        x_in[None], cotangent[None], seg_ids, live_mask, tuple(weights)
    )
    owned_parts = (
        lax.psum_scatter(grads[0], ("dp", "shard"), scatter_dimension=0, tiled=True),
        lax.psum_scatter(grads[1], ("dp", "shard"), scatter_dimension=0, tiled=True),
        lax.psum_scatter(grads[2], ("dp", "shard"), scatter_dimension=0, tiled=True),
        lax.psum_scatter(grads[3], ("dp", "shard"), scatter_dimension=0, tiled=True),
        lax.psum_scatter(grads[4], ("dp", "shard"), scatter_dimension=1, tiled=True),
    )
    owned = jnp.concatenate([piece.reshape(-1) for piece in owned_parts])
    local_index = jnp.arange(owned.shape[0], dtype=jnp.int32)
    decay = decay_rate * (local_index < share * (4 * D + 2 * FF)).astype(jnp.float32)
    new_params, new_first, new_second = adam(params, first_moment, second_moment, owned, decay)
    return (output[0], grad_input[0], owned, new_params, new_first, new_second)


SWAP = ((0, 1), (1, 0))
TEAM = ("x", "c")
LOW = jnp.bfloat16
TOK = 512
ROW = 128


def swap(values, axis):
    return lax.ppermute(values, axis, SWAP)


def hop_to(piece, hop):
    return lax.ppermute(piece, "z", [(i, (i + hop) % 4) for i in range(4)])


def from_hop(at, hop):
    return lax.rem(at[2] + 4 - hop, 4)


def z_gather(shard):
    return lax.all_gather(shard, "z", axis=0, tiled=True)


def z_reduce(values):
    return lax.psum_scatter(values, "z", scatter_dimension=0, tiled=True)


def team_exchange(values):
    return lax.all_to_all(values, TEAM, 0, 0, tiled=True)


def team_gather(own, dep=None):
    near = swap(own, "x")
    onward = near if dep is None else after(near, dep)
    beside = swap(own, "c")
    return (own, near, beside, swap(onward, "c"))


def team_reduce(keep, send):
    recv = swap(send, "c")
    away = (keep[ROW:] + recv[ROW:]).astype(LOW)
    near = swap(away, "x")
    return (keep, recv, near)


def team_total(keep, recv, near):
    return keep[:ROW] + recv[:ROW] + near.astype(jnp.float32)


def sds(shape, dtype=jnp.float32):
    return jax.ShapeDtypeStruct(shape, dtype)


def after(value, dep):
    return lax.optimization_barrier((value, dep))[0]


def call(kernel, outs, at, operands, scratch=()):
    n_in, n_out = len(operands), len(outs)

    def staged(at_ref, *refs):
        hbm_in, hbm_out = refs[:n_in], refs[n_in : n_in + n_out]
        ins = refs[n_in + n_out : 2 * n_in + n_out]
        results = refs[2 * n_in + n_out : 2 * (n_in + n_out)]
        in_sems, out_sems = refs[-2:]
        tmp = refs[2 * (n_in + n_out) : -2]
        loads = [pltpu.make_async_copy(hbm_in[i], ins[i], in_sems.at[i]) for i in range(n_in)]
        stores = [pltpu.make_async_copy(results[i], hbm_out[i], out_sems.at[i]) for i in range(n_out)]
        waited, sent = set(), set()
        for load in loads:
            load.start()

        def ready(*which):
            for i in which or range(n_in):
                if i not in waited:
                    waited.add(i)
                    loads[i].wait()

        def flush(*which):
            for i in which or range(n_out):
                if i not in sent:
                    sent.add(i)
                    stores[i].start()

        kernel(at_ref, ins, results, tmp, ready, flush)
        ready()
        flush()
        for store in stores:
            store.wait()

    hbm = pl.BlockSpec(memory_space=pl.ANY)
    return pl.pallas_call(
        staged,
        out_shape=outs,
        in_specs=[pl.BlockSpec(memory_space=pltpu.SMEM)] + [hbm] * n_in,
        out_specs=(hbm,) * n_out,
        scratch_shapes=[pltpu.VMEM(v.shape, v.dtype) for v in operands]
        + [pltpu.VMEM(v.shape, v.dtype) for v in outs]
        + list(scratch)
        + [pltpu.SemaphoreType.DMA((n_in,)), pltpu.SemaphoreType.DMA((n_out,))],
        compiler_params=pltpu.CompilerParams(vmem_limit_bytes=60 << 20),
    )(at, *operands)


def head_lanes():
    return lax.broadcasted_iota(jnp.int32, (ROW, 128), 1) < HEAD_DIM


def lane_group(rows):
    return lax.broadcasted_iota(jnp.int32, (rows, 128), 1) // 32


def allowed_block(seg_ref, block):
    query_at = lax.broadcasted_iota(jnp.int32, (ROW, ROW), 0)
    key_at = lax.broadcasted_iota(jnp.int32, (ROW, ROW), 1)
    seg_row = seg_ref[block : block + 1, :].astype(jnp.float32)
    seg_col = jnp.sum(jnp.where(query_at == key_at, seg_row, 0.0), axis=1, keepdims=True)
    return (seg_col == seg_row) & (query_at >= key_at)


def scores_of(query_low, key_low, allowed):
    return jnp.where(allowed, matmul_nt(query_low, key_low) * score_scale, neg_large)


def forward_kernel(at, ins, outs, tmp, ready, flush):
    x_ref, seg_ref = ins[:2]
    vec_ref, weight_ref, out_ref, normed_ref, qkv_ref, att_ref, keep_ref, send_ref = outs
    y_pos, team = at[0], at[1]
    group = lane_group(16)
    vec_ref[...] = jnp.zeros_like(vec_ref)
    for index in range(8):
        ready(2 + index)
        ref, side = ins[2 + index], (y_pos if index < 4 else 1 - y_pos)
        z = from_hop(at, index % 4)
        base = side * 512
        for t in range(4):
            start = pl.multiple_of(base + t * 128 + z * 32, 32)
            weight_ref[pl.ds(start, 32), :] = ref[t * 32 : (t + 1) * 32, :]
        top = pl.multiple_of(side * 128 + z * 32, 32)
        out_ref[pl.ds(top, 32), 0:768] = ref[128:160, :]
        out_ref[pl.ds(top, 16), 768:1024] = ref[160:176, 0:256]
        out_ref[pl.ds(pl.multiple_of(top + 16, 16), 16), 768:1024] = ref[160:176, 256:512]
        piece = ref[160:176, 512:640].astype(jnp.float32)
        for t in range(4):
            lanes = pl.ds(pl.multiple_of(base + t * 128, 128), 128)
            turned = pltpu.roll(piece, lax.rem((z - t + 4) * 32, 128), 1)
            vec_ref[:, lanes] = jnp.where(group == z, turned, vec_ref[:, lanes])
    flush(0, 1, 2)
    ready(0, 1)
    gain, shift_row = vec_ref[0:1, :], vec_ref[1:2, :]
    for block in range(4):
        rows = slice(block * ROW, (block + 1) * ROW)
        value, _, _ = normalize(x_ref[rows, :].astype(jnp.float32), gain, shift_row)
        normed_ref[rows, :] = value.astype(LOW)
    for block in range(4):
        rows = slice(block * ROW, (block + 1) * ROW)
        mixed = matmul(normed_ref[rows, :], weight_ref[...])
        for pair in range(2):
            lanes = pl.ds(pl.multiple_of(pair * 512 + team * 128, 128), 128)
            for which in range(3):
                cols = slice(which * 256 + pair * 128, which * 256 + (pair + 1) * 128)
                piece = mixed[:, cols]
                if which == 0:
                    piece = piece + vec_ref[2:3, lanes]
                if which == 2:
                    piece = piece + vec_ref[3:4, lanes]
                qkv_ref[rows, cols] = piece.astype(LOW)
    flush(3, 4)
    first = head_lanes()
    for block in range(4):
        rows = slice(block * ROW, (block + 1) * ROW)
        allowed = allowed_block(seg_ref, block)
        for pair in range(2):
            query, key, value = (
                qkv_ref[rows, w * 256 + pair * 128 : w * 256 + (pair + 1) * 128] for w in range(3)
            )
            heads = []
            for mask in (first, ~first):
                scores = scores_of(jnp.where(mask, query, jnp.zeros_like(query)), key, allowed)
                row_max = jnp.max(scores, axis=-1, keepdims=True)
                exp_scores = jnp.exp(scores - row_max)
                row_total = jnp.sum(exp_scores, axis=-1, keepdims=True)
                heads.append(matmul((exp_scores / row_total).astype(LOW), value))
            att_ref[rows, pair * 128 : (pair + 1) * 128] = jnp.where(first, heads[0], heads[1]).astype(LOW)
    send_ref[...] = matmul(att_ref[256:512, :], out_ref[...])
    flush(5, 7)
    keep_ref[...] = matmul(att_ref[0:256, :], out_ref[...])


def split_kernel(at, ins, outs, tmp, ready, flush):
    left_ref, own_ref, far_ref = ins
    keep_ref, send_ref = outs
    depth = own_ref.shape[0]
    near = pl.ds(pl.multiple_of(at[0] * depth, depth), depth)
    away = pl.ds(pl.multiple_of((1 - at[0]) * depth, depth), depth)
    ready()
    for which, ref, base in ((1, send_ref, 256), (0, keep_ref, 0)):
        rows = slice(base, base + 256)
        ref[...] = matmul(left_ref[rows, near], own_ref[...]) + matmul(left_ref[rows, away], far_ref[...])
        flush(which)


def residual_kernel(at, ins, outs, tmp, ready, flush):
    x_ref, keep_ref, recv_ref, near_ref, vec_ref = ins
    res_ref, low_ref = outs
    ready()
    total = team_total(keep_ref, recv_ref, near_ref[...])
    residual = x_ref[...].astype(jnp.float32) + total + vec_ref[4:5, :]
    res_ref[...] = residual
    value, _, _ = normalize(residual, vec_ref[5:6, :], vec_ref[6:7, :])
    low_ref[...] = value.astype(LOW)


def up_kernel(at, ins, outs, tmp, ready, flush):
    n0, n1, n2, n3, own_ref, far_ref, vec_ref, uplow_ref = ins
    team = at[1]
    team_ref, weight_ref, hidden_ref, slope_ref, grad_ref = outs
    ready(4, 5, 6, 0, 1, 2, 3)
    y_pos = at[0]
    for block, ref in enumerate((n0, n1, n2, n3)):
        team_ref[block * ROW : (block + 1) * ROW, :] = ref[...]
    for ref, side in ((own_ref, y_pos), (far_ref, 1 - y_pos)):
        for z in range(4):
            for t in range(4):
                start = pl.multiple_of(side * 512 + t * 128 + z * 32, 32)
                weight_ref[pl.ds(start, 32), :] = ref[z, t * 32 : (t + 1) * 32, :]
    flush(0, 1)
    bias_lanes = pl.ds(pl.multiple_of((team % 2) * 512, 512), 512)
    bias = jnp.concatenate([vec_ref[pl.ds(7 + 2 * side + team // 2, 1), bias_lanes] for side in range(2)], axis=1)
    for block in range(4):
        rows = slice(block * ROW, (block + 1) * ROW)
        pre_act = matmul(team_ref[rows, :], weight_ref[...]) + bias
        act_value, act_slope = gelu_parts(pre_act)
        hidden_ref[rows, :] = act_value.astype(LOW)
        slope_ref[rows, :] = act_slope
    flush(2, 3)
    ready(7)
    for side in range(2):
        grad = matmul_tn(hidden_ref[:, side * 512 : (side + 1) * 512], uplow_ref[...]).astype(LOW)
        for z in range(4):
            grad_ref[z, side] = grad[z * 128 : (z + 1) * 128, :]


def down_kernel(at, ins, outs, tmp, ready, flush):
    uplow_ref, own_ref, far_ref, slope_ref, weight_ref = ins
    pre_ref, sum_ref, keep_ref, send_ref = outs
    ready(0, 1, 2, 3)
    y_pos = at[0]
    sum_ref[...] = jnp.zeros_like(sum_ref)
    for ref, side in ((own_ref, y_pos), (far_ref, 1 - y_pos)):
        cols = pl.ds(pl.multiple_of(side * 512, 512), 512)
        for block in range(4):
            rows = slice(block * ROW, (block + 1) * ROW)
            grad_pre = matmul_nt(uplow_ref[rows, :], ref[...]) * slope_ref[rows, cols]
            pre_ref[rows, cols] = grad_pre.astype(LOW)
            sum_ref[0:1, cols] += jnp.sum(grad_pre, axis=0, keepdims=True)
    flush(0, 1)
    ready(4)
    send_ref[...] = matmul_nt(pre_ref[256:512, :], weight_ref[...])
    flush(3)
    keep_ref[...] = matmul_nt(pre_ref[0:256, :], weight_ref[...])


def spread(at, grad_ref, mine_ref, theirs_ref):
    y_pos = at[0]
    for z in range(4):
        for t in range(4):
            near = pl.multiple_of(y_pos * 512 + t * 128 + z * 32, 32)
            away = pl.multiple_of((1 - y_pos) * 512 + t * 128 + z * 32, 32)
            mine_ref[z, t * 32 : (t + 1) * 32, :] = grad_ref[pl.ds(near, 32), :]
            theirs_ref[z, t * 32 : (t + 1) * 32, :] = grad_ref[pl.ds(away, 32), :].astype(LOW)


def up_grad_kernel(at, ins, outs, tmp, ready, flush):
    team_ref, pre_ref = ins
    mine_ref, theirs_ref = outs
    grad_ref, = tmp
    ready()
    grad_ref[...] = matmul_tn(team_ref[...], pre_ref[...])
    spread(at, grad_ref, mine_ref, theirs_ref)


def residual_back_kernel(at, ins, outs, tmp, ready, flush):
    res_ref, keep_ref, recv_ref, near_ref, up_ref, vec_ref = ins
    grad_ref, low_ref, rows_ref = outs
    ready()
    _, scaled, inverse = normalize(res_ref[...], vec_ref[5:6, :], vec_ref[6:7, :])
    grad_normed = team_total(keep_ref, recv_ref, near_ref[...])
    upstream = up_ref[...]
    grad = upstream + normalize_back(grad_normed, scaled, inverse, vec_ref[5:6, :])
    grad_ref[...] = grad
    low_ref[...] = grad.astype(LOW)
    total = lambda value: jnp.sum(value, axis=0, keepdims=True)
    rows_ref[...] = jnp.zeros_like(rows_ref)
    rows_ref[0:1, :] = total(grad)
    rows_ref[1:2, :] = total(grad_normed * scaled)
    rows_ref[2:3, :] = total(grad_normed)
    rows_ref[3:4, :] = total(upstream)


def out_grad_kernel(at, ins, outs, tmp, ready, flush):
    att_ref = ins[4]
    mine_ref, theirs_ref = outs
    ready(4)
    for ref, side in ((theirs_ref, 1 - at[0]), (mine_ref, at[0])):
        cols = pl.ds(pl.multiple_of(side * 128, 128), 128)
        total = jnp.zeros((128, D), jnp.float32)
        for block in range(4):
            ready(block)
            total = total + matmul_tn(att_ref[block * ROW : (block + 1) * ROW, cols], ins[block][...])
        ref[...] = total.astype(ref.dtype)


def backward_kernel(at, ins, outs, tmp, ready, flush):
    out_ref, qkv_ref, seg_ref, normed_ref, x_ref, weight_ref, rows_ref, pre_ref = ins[4:]
    keep_ref, send_ref = outs[8:]
    mixed_ref, grad_ref, att_ref, vec_ref = tmp
    team = at[1]
    ready(4)
    for block in range(4):
        ready(block)
        att_ref[block * ROW : (block + 1) * ROW, :] = matmul_nt(ins[block][...], out_ref[...]).astype(LOW)
    ready(5, 6, 10, 11)
    vec_ref[...] = jnp.zeros_like(vec_ref)
    vec_ref[4:7, :] = rows_ref[0:3, :]
    vec_ref[11:12, :] = rows_ref[3:4, :]
    for side in range(2):
        at_row = pl.ds(7 + 2 * side + team // 2, 1)
        vec_ref[at_row, pl.ds(pl.multiple_of((team % 2) * 512, 512), 512)] = pre_ref[0:1, side * 512 : (side + 1) * 512]
    first = head_lanes()
    for pair in range(2):
        query_sum = jnp.zeros((1, 128), jnp.float32)
        value_sum = jnp.zeros((1, 128), jnp.float32)
        for block in range(4):
            rows = slice(block * ROW, (block + 1) * ROW)
            allowed = allowed_block(seg_ref, block)
            query, key, value = (
                qkv_ref[rows, w * 256 + pair * 128 : w * 256 + (pair + 1) * 128] for w in range(3)
            )
            grad_att = att_ref[rows, pair * 128 : (pair + 1) * 128]
            parts = []
            for mask in (first, ~first):
                scores = scores_of(jnp.where(mask, query, jnp.zeros_like(query)), key, allowed)
                row_max = jnp.max(scores, axis=-1, keepdims=True)
                log_total = row_max + jnp.log(jnp.sum(jnp.exp(scores - row_max), axis=-1, keepdims=True))
                probability = jnp.where(allowed, jnp.exp(scores - log_total), 0.0)
                grad_prob = matmul_nt(jnp.where(mask, grad_att, jnp.zeros_like(grad_att)), value)
                grad_value = matmul_tn(probability.astype(LOW), grad_att)
                row_dot = jnp.sum(probability * grad_prob, axis=-1, keepdims=True)
                score_low = (probability * (grad_prob - row_dot)).astype(LOW)
                parts.append(
                    (matmul(score_low, key) * score_scale, matmul_tn(score_low, query) * score_scale, grad_value)
                )
            for which in range(3):
                merged = jnp.where(first, parts[0][which], parts[1][which])
                mixed_ref[rows, which * 256 + pair * 128 : which * 256 + (pair + 1) * 128] = merged.astype(LOW)
                if which == 0:
                    query_sum = query_sum + jnp.sum(merged, axis=0, keepdims=True)
                if which == 2:
                    value_sum = value_sum + jnp.sum(merged, axis=0, keepdims=True)
        lanes = pl.ds(pl.multiple_of(pair * 512 + team * 128, 128), 128)
        vec_ref[2:3, lanes] = query_sum
        vec_ref[3:4, lanes] = value_sum
    ready()
    send_ref[...] = matmul_nt(mixed_ref[256:512, :], weight_ref[...])
    keep_ref[...] = matmul_nt(mixed_ref[0:256, :], weight_ref[...])
    flush(8, 9)
    grad_ref[...] = matmul_tn(normed_ref[...], mixed_ref[...])
    gain_sum = jnp.zeros((1, D), jnp.float32)
    shift_sum = jnp.zeros((1, D), jnp.float32)
    for block in range(4):
        rows = slice(block * ROW, (block + 1) * ROW)
        _, scaled, _ = normalize(x_ref[rows, :].astype(jnp.float32), 1.0, 0.0)
        source, at_row = (keep_ref, block) if block < 2 else (send_ref, block - 2)
        partial = source[at_row * ROW : (at_row + 1) * ROW, :]
        gain_sum = gain_sum + jnp.sum(partial * scaled, axis=0, keepdims=True)
        shift_sum = shift_sum + jnp.sum(partial, axis=0, keepdims=True)
    vec_ref[0:1, :] = gain_sum
    vec_ref[1:2, :] = shift_sum
    group = lane_group(16)
    for hop in (2, 1, 3, 0):
        z = lax.rem(at[2] + hop, 4)
        for index, side in ((4 + hop, 1 - at[0]), (hop, at[0])):
            for t in range(4):
                start = pl.multiple_of(side * 512 + t * 128 + z * 32, 32)
                outs[index][t * 32 : (t + 1) * 32, :] = grad_ref[pl.ds(start, 32), :].astype(outs[index].dtype)
            tile = jnp.zeros((16, 128), jnp.float32)
            for t in range(4):
                piece = vec_ref[:, pl.ds(pl.multiple_of(side * 512 + t * 128, 128), 128)]
                turned = pltpu.roll(piece, lax.rem((t - z + 4) * 32, 128), 1)
                tile = jnp.where(group == t, turned, tile)
            outs[index][128:144, 0:128] = tile.astype(outs[index].dtype)
            outs[index][128:144, 128:768] = jnp.zeros((16, 640), outs[index].dtype)
            flush(index)


def step_rows(params_ref, first_ref, second_ref, grad_ref, new_refs, start, count, chunk, decay):
    def visit(index, carry):
        rows = pl.ds(pl.multiple_of(start + index * chunk, 8), chunk)
        outs = adam(params_ref[rows, :], first_ref[rows, :], second_ref[rows, :], grad_ref[rows, :], decay)
        for ref, value in zip(new_refs, outs):
            ref[rows, :] = value
        return carry

    lax.fori_loop(0, count // chunk, visit, 0)


def run_copies(pairs, sems, base):
    copies = [pltpu.make_async_copy(src, dst, sems.at[base + i]) for i, (src, dst) in enumerate(pairs)]
    for copy in copies:
        copy.start()
    for copy in copies:
        copy.wait()


def early_kernel(at, p_hbm, m_hbm, v_hbm, down_hbm, *refs):
    hbm_outs = refs[:4]
    p_ref, m_ref, v_ref, down_ref, g_ref, np_ref, nm_ref, nv_ref, sems = refs[4:]
    part = lambda ref: ref.at[pl.ds(2048, 1024), :]
    pairs = [(down_hbm, down_ref)]
    pairs.extend((part(hbm), ref) for hbm, ref in ((p_hbm, p_ref), (m_hbm, m_ref), (v_hbm, v_ref)))
    run_copies(pairs, sems, 0)
    for j in range(8):
        g_ref[pl.ds(j, 128, stride=8), :] = down_ref[:, j * 128 : (j + 1) * 128].astype(jnp.float32)
    step_rows(p_ref, m_ref, v_ref, g_ref, (np_ref, nm_ref, nv_ref), 0, 1024, 128, decay_rate)
    run_copies([(src, part(dst)) for src, dst in zip((g_ref, np_ref, nm_ref, nv_ref), hbm_outs)], sems, 4)


def late_kernel(at, p_hbm, m_hbm, v_hbm, qkv_hbm, out_hbm, *refs):
    hbm_outs = refs[4:8]
    p_ref, m_ref, v_ref, qkv_ref, out_ref, g_ref, np_ref, nm_ref, nv_ref, sems = refs[8:]
    spans = lambda ref, hbm: (
        (hbm.at[pl.ds(0, 2048), :], ref.at[pl.ds(0, 2048), :]),
        (hbm.at[pl.ds(3072, 3), :], ref.at[pl.ds(2048, 3), :]),
    )
    pairs = [(qkv_hbm, qkv_ref), (out_hbm, out_ref)]
    for hbm, ref in ((p_hbm, p_ref), (m_hbm, m_ref), (v_hbm, v_ref)):
        pairs.extend(spans(ref, hbm))
    run_copies(pairs, sems, 0)
    for g in range(6):
        for t in range(4):
            g_ref[pl.ds(g * 4 + t, 32, stride=24), :] = qkv_ref[t, 0:32, g * 128 : (g + 1) * 128].astype(jnp.float32)
    for j in range(8):
        g_ref[pl.ds(768 + j, 32, stride=8), :] = out_ref[:, j * 128 : (j + 1) * 128].astype(jnp.float32)
    for t in range(4):
        for part in range(8):
            flat = 1024 + (part // 4) * 16 + t * 4 + part % 4
            if part < 6:
                value = qkv_ref[t, 48:80, part * 128 : (part + 1) * 128]
                g_ref[pl.ds(flat, 32, stride=32), :] = value.astype(jnp.float32)
            else:
                for half in range(2):
                    lane = half * 256 + (part - 6) * 128
                    value = qkv_ref[t, 80:96, lane : lane + 128]
                    g_ref[pl.ds(flat + half * 512, 16, stride=32), :] = value.astype(jnp.float32)
    total = jnp.zeros((16, 128), jnp.float32)
    for t in range(4):
        total = total + qkv_ref[t, 32:48, 0:128].astype(jnp.float32)
    group = lane_group(1)
    turned = [pltpu.roll(total, q * 32, 1) if q else total for q in range(4)]
    for r in range(3):
        row = jnp.zeros((1, 128), jnp.float32)
        for q in range(4):
            row = jnp.where(group == q, turned[q][4 * r + q : 4 * r + q + 1, :], row)
        g_ref[2048 + r : 2049 + r, :] = row
    new_refs = (np_ref, nm_ref, nv_ref)
    step_rows(p_ref, m_ref, v_ref, g_ref, new_refs, 0, 2048, 128, decay_rate)
    tail = slice(2048, 2051)
    outs = adam(p_ref[tail, :], m_ref[tail, :], v_ref[tail, :], g_ref[tail, :], 0.0)
    for ref, value in zip(new_refs, outs):
        ref[tail, :] = value
    pairs = []
    for hbm, ref in zip(hbm_outs, (g_ref,) + new_refs):
        pairs.extend((src, dst) for dst, src in spans(ref, hbm))
    run_copies(pairs, sems, 8)


def adam_call(kernel, at, arrays, previous, rows, extra_sems):
    hbm = pl.BlockSpec(memory_space=pltpu.HBM)
    operands = tuple(arrays) + tuple(previous)
    grads = [pltpu.VMEM(v.shape, v.dtype) for v in arrays[3:]]
    block = pltpu.VMEM((rows, 128), jnp.float32)
    return pl.pallas_call(
        kernel,
        out_shape=tuple(sds(arrays[0].shape) for _ in range(4)),
        in_specs=[pl.BlockSpec(memory_space=pltpu.SMEM)] + [hbm] * len(operands),
        out_specs=(hbm,) * 4,
        scratch_shapes=[block] * 3 + grads + [block] * 4 + [pltpu.SemaphoreType.DMA((extra_sems,))],
        input_output_aliases={1 + len(arrays) + i: i for i in range(len(previous))},
        compiler_params=pltpu.CompilerParams(vmem_limit_bytes=60 << 20),
    )(at, *operands)


def join_kernel(at, ins, outs, tmp, ready, flush):
    mine_ref, recv_ref, r1, r2, r3, up_ref = ins
    pay_ref, = outs
    ready()
    total = mine_ref[...] + recv_ref[...].astype(jnp.float32)
    for ref in (r1, r2, r3):
        total = total + ref[...].astype(jnp.float32)
    for t in range(4):
        pay_ref[t, 0:32, :] = total[t * 32 : (t + 1) * 32, :].astype(LOW)
        tile = total[128:144, 0:128]
        pay_ref[t, 32:48, 0:128] = (pltpu.roll(tile, 128 - t * 32, 1) if t else tile).astype(LOW)
        pay_ref[t, 32:48, 128:768] = jnp.zeros((16, 640), LOW)
        pay_ref[t, 48:80, :] = up_ref[t * 32 : (t + 1) * 32, 0:768]
        pay_ref[t, 80:96, 0:256] = up_ref[t * 32 : t * 32 + 16, 768:1024]
        pay_ref[t, 80:96, 256:512] = up_ref[t * 32 + 16 : t * 32 + 32, 768:1024]
        pay_ref[t, 80:96, 512:768] = jnp.zeros((16, 256), LOW)


def team_body(*arrays):
    return team_step(*arrays)


def team_step(x_in, cotangent, params, first_moment, second_moment, seq_lengths, seq_device):
    rows = x_in.shape[0]
    share = D // 32
    y_pos = lax.axis_index("y")
    x_pos = lax.axis_index("x")
    c_pos = lax.axis_index("c")
    z_pos = lax.axis_index("z")
    team_pos = x_pos * 2 + c_pos
    at = jnp.stack([y_pos, team_pos, z_pos]).astype(jnp.int32)

    qkv_part, out_part, up_part, down_part, vec_part = local_pieces(params.astype(LOW), share)
    qkv_send = qkv_part.reshape(share, 6, 4, 128).transpose(2, 0, 1, 3).reshape(4, share, 768)
    vec_row = jnp.broadcast_to(jnp.pad(vec_part, ((0, 4), (0, 736)))[None], (4, 16, 768))
    qkv_team = team_exchange(jnp.concatenate([qkv_send, vec_row], axis=1))
    vec_team = qkv_team[:, share:, :32].transpose(1, 0, 2).reshape(16, 128)
    rest = jnp.concatenate(
        [out_part[:16, 768:], out_part[16:, 768:], vec_team, jnp.zeros((16, 128), LOW)], axis=1
    )
    qkv_shard = jnp.concatenate([qkv_team[:, :share].reshape(4 * share, 768), out_part[:, :768], rest])
    up_send = up_part.reshape(share, 2, 4, 512).transpose(2, 0, 1, 3).reshape(4, share, 1024)
    qkv_near = [qkv_shard] + [hop_to(qkv_shard, hop) for hop in (1, 2, 3)]
    qkv_far = [swap(qkv_shard, "y")]
    qkv_far = qkv_far + [swap(piece, "y") for piece in qkv_near[1:]]
    up_team = team_exchange(after(up_send, qkv_shard)).reshape(4 * share, 1024)
    up_own = z_gather(after(up_team, qkv_near[1:])).reshape(4, 4 * share, 1024)
    up_far = swap(up_own, "y")
    down_own = z_gather(after(down_part, (up_team, qkv_near[1:])))

    steps = jnp.arange(2, dtype=jnp.int32)
    team_devices = (
        ((y_pos * 2 + (x_pos ^ steps[None, :])) * 2 + (c_pos ^ steps[:, None])) * 4 + z_pos
    ).reshape(4)
    seg_ids, live_mask = segments(seq_lengths, seq_device, team_devices.astype(jnp.int32), rows)

    upstream = cotangent * live_mask[0][:, None].astype(jnp.float32)
    token_pack = after(jnp.stack([x_in, upstream.astype(LOW)]), up_team)
    tokens = jnp.stack(team_gather(token_pack, qkv_near[1:]))
    x_team = tokens[:, 0].reshape(TOK, D)
    up_low = tokens[:, 1].reshape(TOK, D)

    vectors, qkv_weight, out_weight, normed1, qkv_low, attended, keep, send = call(
        forward_kernel,
        (
            sds((16, D)), sds((D, 768), LOW), sds((256, D), LOW), sds((TOK, D), LOW),
            sds((TOK, 768), LOW), sds((TOK, 256), LOW), sds((256, D)), sds((256, D)),
        ),
        at,
        (x_team, seg_ids, *qkv_near, *qkv_far),
    )
    keep, recv, near = team_reduce(keep, send)
    residual, normed2 = call(
        residual_kernel, (sds((rows, D)), sds((rows, D), LOW)), at, (x_in, keep, recv, near, vectors)
    )
    norm_blocks = team_gather(normed2)
    down_far = swap(after(down_own, normed2), "y")
    normed2, up_weight, hidden, slope, down_grad = call(
        up_kernel,
        (
            sds((TOK, D), LOW), sds((D, 1024), LOW), sds((TOK, 1024), LOW), sds((TOK, 1024)),
            sds((4, 2, 128, D), LOW),
        ),
        at,
        (*norm_blocks, up_own, up_far, vectors, up_low),
    )
    down_sides = z_reduce(down_grad.reshape(1024, D)).reshape(2, 128, D)
    pre_low, pre_sum, keep, send = call(
        down_kernel,
        (sds((TOK, 1024), LOW), sds((8, 1024)), sds((256, D)), sds((256, D))),
        at,
        (up_low, down_own, down_far, slope, up_weight),
    )
    keep, recv, near = team_reduce(keep, send)
    up_mine, up_theirs = call(
        up_grad_kernel,
        (sds((4, 4 * share, 1024)), sds((4, 4 * share, 1024), LOW)),
        at,
        (normed2, pre_low),
        [pltpu.VMEM((D, 1024), jnp.float32)],
    )
    up_recv = swap(up_theirs, "y")
    grad_residual, res_low, row_sums = call(
        residual_back_kernel,
        (sds((rows, D)), sds((rows, D), LOW), sds((8, D))),
        at,
        (residual, keep, recv, after(near, up_theirs), upstream, vectors),
    )
    y_sum = lambda mine, recv: (mine + recv.astype(jnp.float32)).astype(LOW)
    res_blocks = team_gather(res_low)
    out_mine, out_theirs = call(out_grad_kernel, (sds((128, D)), sds((128, D), LOW)), at, (*res_blocks, attended))
    out_recv = swap(out_theirs, "y")
    out_keep, out_send = call(
        split_kernel, (sds((256, D)), sds((256, D))), at,
        (after(hidden, out_theirs), down_own, down_far),
    )
    up_pay = y_sum(after(up_mine, out_send), up_recv).reshape(TOK, D)
    up_sum = z_reduce(up_pay)
    down_recv = swap(lax.dynamic_index_in_dim(down_sides, 1 - y_pos, 0, keepdims=False), "y")
    *qkv_parts, keep, send = call(
        backward_kernel,
        (sds((144, 768)),) * 4 + (sds((144, 768), LOW),) * 4 + (sds((256, D)), sds((256, D))),
        at,
        (*res_blocks, out_weight, qkv_low, seg_ids, normed1, x_team, qkv_weight, row_sums, pre_sum),
        [
            pltpu.VMEM((TOK, 768), LOW), pltpu.VMEM((D, 768), jnp.float32),
            pltpu.VMEM((TOK, 256), LOW), pltpu.VMEM((16, D), jnp.float32),
        ],
    )
    first_recv = swap(qkv_parts[4 + 2], "y")
    rest_recv = [swap(qkv_parts[4 + hop], "y") for hop in (1, 3, 0)]
    qkv_recv = (rest_recv[2], rest_recv[0], first_recv, rest_recv[1])
    down_mine = lax.dynamic_index_in_dim(down_sides, y_pos, 0, keepdims=False)
    down_sum = down_mine.astype(jnp.float32) + after(down_recv, qkv_parts[4]).astype(jnp.float32)
    out_sum = z_reduce(y_sum(after(out_mine, qkv_parts[4]), out_recv))
    joined = {hop: (qkv_parts[hop] + qkv_recv[hop].astype(jnp.float32)).astype(LOW) for hop in (1, 2, 3)}
    turned = [hop_to(joined[2], 2)]
    turned.append(hop_to(joined[1], 1))
    turned.append(hop_to(joined[3], 3))

    final_keep, final_send = keep, send
    output = residual + team_total(*team_reduce(out_keep, out_send)) + vectors[7 + FF // D]
    grad_normed1 = team_total(*team_reduce(final_keep, final_send))
    _, scaled1, inverse1 = normalize(x_in.astype(jnp.float32), vectors[0], vectors[1])
    grad_input = grad_residual + normalize_back(grad_normed1, scaled1, inverse1, vectors[0])

    state = tuple(v.reshape(-1, 128) for v in (params, first_moment, second_moment))
    early = adam_call(early_kernel, at, (*state, down_sum), (), 1024, 8)
    (qkv_pay,) = call(
        join_kernel, (sds((4, 96, 768), LOW),), at, (qkv_parts[0], after(qkv_recv[0], early[0]), *turned, up_sum)
    )
    qkv_back = team_exchange(qkv_pay)
    final = adam_call(late_kernel, at, (*state, qkv_back, out_sum), early, 2056, 16)
    owned, new_params, new_first, new_second = (v.reshape(-1) for v in final)
    return (output, grad_input, owned, new_params, new_first, new_second)


def solution(mesh):
    shape = dict(mesh.shape)
    if shape["dp"] == 8 and shape["shard"] == 4:
        mesh = Mesh(mesh.devices.reshape(2, 2, 2, 4), ("y", "x", "c", "z"))
        axes, step = ("y", "x", "c", "z"), team_body
    else:
        axes, step = ("dp", "shard"), body
    mapped = jax.shard_map(
        step,
        mesh=mesh,
        in_specs=(P(axes, None), P(axes, None), P(axes), P(axes), P(axes), P(), P()),
        out_specs=(P(axes, None), P(axes, None), P(axes), P(axes), P(axes), P(axes)),
        check_vma=False,
    )
    if step is body:
        return mapped
    return mapped
```
